128 devices in a mesh: row: 16 (over z, x_lo, core), col: 8 (over y, x_hi).
Axes of the slice: x: 4 (x_hi: 2, x_lo: 2; x = x_hi * 2 + x_lo), y: 4, z: 4, core: 2. Of those that a mesh axis runs over, the one named last changes fastest.
Arguments:
- genotypes: bfloat16 [5120, 16384], P(None, ('row', 'col')), may hold values from -5 to 5
- running: float32 [16384, 16, 8, 128], P('row', None, 'col'), as said below
- grid_map: int32 [16], replicated, may hold values from 0 to 15, each once
Outputs:
- factored: float32 [16, 16, 64, 16, 8, 128], P(None, 'row', None, None, 'col')
The draws below stay inside these ranges and needn't reach their ends.
Inputs may be any that keep to these rules, and one draw needn't show every extreme that they name: running is symmetric, and in its first 128 rows each diagonal entry exceeds the sum of the magnitudes of the row's other entries among the first 128 columns. grid_map holds each of its values once.
All inputs are finite; a program needn't handle non-finite values.
Results may differ from the reference program's by a relative error of at most 0.0003.
Values may be sent and summed in bfloat16 or wider, within the bound.
No kernel may reach another device: no remote copies, remote signals or barrier semaphores. Data moves between devices by JAX's collectives and lax.ppermute only.
A program may use at most 128 MiB of HBM per device.

```python
import jax
import jax.numpy as jnp
from jax import lax

N = 16384
M = 5120
NB = 128
SHARD = 128
SUB = 64
N_ROW = 16
N_COL = 8


def draw_genotypes(key, part):
    first_key = jax.random.fold_in(jax.random.fold_in(key, 17), 0)
    values = jax.random.normal(first_key, (M, N), jnp.float32)
    return jnp.clip(values, -5.0, 5.0).astype(jnp.bfloat16)


def draw_running(key, part):
    first_key = jax.random.fold_in(key, 0)
    third_key = jax.random.fold_in(key, 2)
    noise = jax.random.uniform(first_key, (N, N), jnp.float32, -0.01, 0.01)
    index = jnp.arange(N)
    symmetric = jnp.where(index[:, None] <= index[None, :], noise, noise.T)
    diagonal = jax.random.uniform(third_key, (N,), jnp.float32, 2.0, 3.0)
    symmetric = jnp.where(index[:, None] == index[None, :], diagonal[:, None], symmetric)
    return symmetric.reshape(N, N_ROW, N_COL, N // (N_ROW * N_COL))


def setup_inputs(seed: int = 0) -> dict:
    arg_keys = jax.random.split(jax.random.key(seed), 4)
    genotypes = draw_genotypes(jax.random.fold_in(arg_keys[3], 71), 0)
    running = draw_running(jax.random.fold_in(arg_keys[3], 71), 0)
    grid_map = jax.random.permutation(arg_keys[2], N_ROW).astype(jnp.int32)
    return dict(genotypes=genotypes, running=running, grid_map=grid_map)


def reference(genotypes, running, grid_map):
    values = genotypes.astype(jnp.float32)
    product = jnp.dot(values.T, values, precision=lax.Precision.HIGHEST)
    updated = running.reshape(N, N) + product * (1.0 / M)
    lower = jnp.linalg.cholesky(updated[:NB, :NB])
    factor = lax.linalg.triangular_solve(lower, updated[:, :NB], left_side=False, lower=True, transpose_a=True)
    trail = updated - jnp.dot(factor, factor.T, precision=lax.Precision.HIGHEST)
    row_pos = jnp.arange(N, dtype=jnp.int32)[:, None]
    col_pos = jnp.arange(NB, dtype=jnp.int32)[None, :]
    left_part = jnp.where(row_pos >= col_pos, factor, jnp.zeros_like(factor))
    right_part = jnp.where(row_pos < NB, jnp.zeros_like(trail[:, NB:]), trail[:, NB:])
    finished = jnp.concatenate([left_part, right_part], axis=1)
    tiles = finished.reshape(N_ROW, N_ROW, SUB, N_ROW, N_COL, SHARD)
    inverse_map = jnp.argsort(grid_map).astype(jnp.int32)
    return jnp.take(tiles, inverse_map, axis=1)
```

```python
import jax
import jax.numpy as jnp
from jax import lax
from jax.experimental import pallas as pl
from jax.experimental.pallas import tpu as pltpu
from jax.sharding import PartitionSpec as P

NB = 128
NZ, NX, NC = 4, 2, 2
NY, NH = 4, 2
SLOT_OF_STEP = (0, 2, 3, 1)


def row_perm(dz=0, fx=0, fc=0):
    return [
        ((z * NX + x) * NC + k, (((z + dz) % NZ) * NX + (x ^ fx)) * NC + (k ^ fc))
        for z in range(NZ)
        for x in range(NX)
        for k in range(NC)
    ]


def col_perm(dy=0, fh=0):
    return [(y * NH + h, ((y + dy) % NY) * NH + (h ^ fh)) for y in range(NY) for h in range(NH)]


def ring_gather(shard, axis, perm):
    half = shard.shape[0] // 2
    up = lax.ppermute(shard, axis, perm(1))
    down = lax.ppermute(shard, axis, perm(-1))
    top = lax.ppermute(up[:half], axis, perm(1))
    bottom = lax.ppermute(down[half:], axis, perm(-1))
    return [shard, up, down, jnp.concatenate([top, bottom], axis=0)]


def ring_direct(shard, axis, perm):
    return [shard] + [lax.ppermute(shard, axis, perm(d)) for d in (1, -1, 2)]


def epilogue_kernel(table, running, prod0, prod1, prod2, prod3, row_factor, col_factor, out, *, inv_snp):
    step = pl.program_id(0)
    row_start = table[32 + step]
    panel_device = table[64]
    row_pos = row_start + lax.broadcasted_iota(jnp.int32, (64, 128), 0)
    lane = lax.broadcasted_iota(jnp.int32, (64, 128), 1)
    mine = row_factor[...]
    high = mine.astype(jnp.bfloat16)
    low = (mine - high.astype(jnp.float32)).astype(jnp.bfloat16)
    left = jnp.concatenate([high, high, low], axis=1)
    panel = jnp.where(row_pos >= lane, mine, 0.0)
    for rel in range(16):
        place = table[48 + rel]
        prod = (prod0, prod1, prod2, prod3)[rel // 4]
        begin = (rel % 4) * 128
        outer = lax.dot_general(
            left,
            col_factor[rel * 128 : (rel + 1) * 128, :],
            (((1,), (1,)), ((), ())),
            preferred_element_type=jnp.float32,
        )
        old = running[pl.ds(place, 64, stride=16), :]
        trail = old + prod[:, begin : begin + 128] * inv_snp - outer
        trail = jnp.where(row_pos < NB, 0.0, trail)
        is_panel = jnp.logical_and(panel_device == 1, place == 0)
        out[pl.ds(place, 64, stride=16), :] = jnp.where(is_panel, panel, trail)


def epilogue(table, running, prods, row_factor, col_factor, snp_count):
    rows = 64
    block = pl.BlockSpec((rows, 512), lambda i, t: (t[16 + i], 0))
    return pl.pallas_call(
        lambda *refs: epilogue_kernel(*refs, inv_snp=1.0 / snp_count),
        grid_spec=pltpu.PrefetchScalarGridSpec(
            num_scalar_prefetch=1,
            grid=(16,),
            in_specs=[
                pl.BlockSpec((rows * 16, 128), lambda i, t: (t[i], 0)),
                block,
                block,
                block,
                block,
                pl.BlockSpec((rows, 128), lambda i, t: (t[16 + i], 0)),
                pl.BlockSpec((2048, 384), lambda i, t: (0, 0)),
            ],
            out_specs=pl.BlockSpec((rows * 16, 128), lambda i, t: (i, 0)),
        ),
        out_shape=jax.ShapeDtypeStruct((16 * rows * 16, 128), jnp.float32),
        name="epilogue",
    )(table, running, *prods, row_factor, col_factor)


def on_device(genotypes, running, grid_map):
    row_index = lax.axis_index("row")
    col_index = lax.axis_index("col")
    z, x_lo, core = row_index // (NX * NC), (row_index // NC) % NX, row_index % NC
    y, x_hi = col_index // NH, col_index % NH
    snp_count = genotypes.shape[0]
    inv_snp = 1.0 / snp_count
    contract0 = (((0,), (0,)), ((), ()))

    def dot0(a, b):
        return lax.dot_general(a, b, contract0, preferred_element_type=jnp.float32)

    across = lax.ppermute(genotypes, "col", col_perm(0, 1))
    beside = lax.ppermute(genotypes, "row", row_perm(0, 1, 0))
    y_own = ring_gather(genotypes, "col", col_perm)
    z_own = ring_gather(genotypes, "row", row_perm)
    y_across = ring_gather(across, "col", col_perm)
    z_beside = ring_gather(beside, "row", row_perm)
    mine_rows = jnp.concatenate([s for pair in zip(y_own, y_across) for s in pair], axis=1)
    col_groups = []
    for own, side in zip(z_own, z_beside):
        own_twin = lax.ppermute(own, "row", row_perm(0, 0, 1))
        side_twin = lax.ppermute(side, "row", row_perm(0, 0, 1))
        col_groups.append(jnp.concatenate([own, own_twin, side, side_twin], axis=1))

    leading = running[:NB, 0, 0, :] + dot0(genotypes, genotypes) * inv_snp
    lower = jnp.linalg.cholesky(leading)
    inverse = lax.linalg.triangular_solve(
        lower, jnp.eye(NB, dtype=jnp.float32), left_side=True, lower=True
    )
    heard = sum(lax.ppermute(inverse, "row", [(0, d * NX * NC)]) for d in range(1, NZ))
    inverse = jnp.where(z == 0, inverse, heard)
    heard = lax.ppermute(inverse, "row", [(d * NX * NC, d * NX * NC + NC) for d in range(NZ)])
    inverse = jnp.where(x_lo == 0, inverse, heard)
    heard = lax.ppermute(inverse, "row", [(d * NC, d * NC + 1) for d in range(NZ * NX)])
    inverse = jnp.where(core == 0, inverse, heard)

    steps = jnp.array(SLOT_OF_STEP, jnp.int32)
    slot0 = steps[(0 - z) % NZ]
    lane0 = (x_lo * NC + core) * 128
    first = sum(
        jnp.where(slot0 == t, lax.dynamic_slice_in_dim(g, lane0, 128, 1), jnp.zeros((), g.dtype))
        for t, g in enumerate(col_groups)
    )
    panel = dot0(mine_rows, first).reshape(NY * NH, 128, NB)
    panel = jnp.concatenate(
        [panel[2 * SLOT_OF_STEP[b] : 2 * SLOT_OF_STEP[b] + 2] for b in range(NY)], axis=0
    ).reshape(NY * NH * 128, NB)
    panel = running[:, 0, 0, :] + panel * inv_snp
    factor = lax.dot_general(
        panel,
        inverse,
        (((1,), (1,)), ((), ())),
        precision=lax.Precision.HIGHEST,
        preferred_element_type=jnp.float32,
    )
    own_factor = factor[:128]
    got = sum(
        lax.ppermute(factor[c * 128 : (c + 1) * 128], "col", [(0, c)]) for c in range(1, NY * NH)
    )
    own_factor = jnp.where(col_index == 0, own_factor, got)
    pair = jnp.stack([own_factor, lax.ppermute(own_factor, "col", col_perm(0, 1))])
    row_factor = jnp.concatenate(ring_direct(pair, "col", col_perm), axis=0).reshape(1024, NB)
    pair = jnp.stack([own_factor, lax.ppermute(own_factor, "row", row_perm(0, 1, 0))])
    half = jnp.concatenate(ring_direct(pair, "row", row_perm), axis=0)
    twin = lax.ppermute(half, "row", row_perm(0, 0, 1))
    col_factor = jnp.stack([half, twin], axis=1).reshape(2048, NB)
    high = col_factor.astype(jnp.bfloat16)
    low = (col_factor - high.astype(jnp.float32)).astype(jnp.bfloat16)
    col_factor = jnp.concatenate([high, low, high], axis=1)

    prods = [dot0(mine_rows, g) for g in col_groups]

    inverse_map = jnp.argsort(grid_map).astype(jnp.int32)
    block = inverse_map // 2
    slot = steps[(block // NH - y) % NY] * 2 + ((block % NH) ^ x_hi)
    tile = slot * 2 + inverse_map % 2
    row_start = row_index * 1024 + inverse_map * 64
    step_of_slot = jnp.array([0, 3, 1, 2], jnp.int32)
    rel = jnp.arange(16, dtype=jnp.int32)
    place = (((step_of_slot[rel // 4] + z) % NZ) * NX + (((rel // 2) % 2) ^ x_lo)) * NC + ((rel % 2) ^ core)
    is_col0 = (col_index == 0).astype(jnp.int32)
    table = jnp.concatenate([inverse_map, tile, row_start, place, is_col0[None]]).astype(jnp.int32)

    send = epilogue(table, running.reshape(1024 * 16, 128), prods, row_factor, col_factor, snp_count)
    result = lax.all_to_all(send.reshape(16, 1024, 128), "row", split_axis=0, concat_axis=0, tiled=True)
    return result.reshape(16, 1, 64, 16, 1, 128)


def solution(mesh):
    in_specs = (P(None, ("row", "col")), P("row", None, "col", None), P())
    out_specs = P(None, "row", None, None, "col", None)
    return jax.shard_map(
        on_device, mesh=mesh, in_specs=in_specs, out_specs=out_specs, check_vma=False
    )
```

```python
import jax
import jax.numpy as jnp
from jax import lax
from jax.experimental import pallas as pl
from jax.experimental.pallas import tpu as pltpu
from jax.sharding import PartitionSpec as P

NB = 128
NZ, NX, NC = 4, 2, 2
NY, NH = 4, 2
SLOT_OF_STEP = (0, 2, 3, 1)
STEP_OF_SLOT = (0, 3, 1, 2)
TILE_ROWS = 64
LEVELS = 32767.0
LOG_STEP = 0.6931471805599453 / 64.0


def row_perm(dz=0, fx=0, fc=0):
    return [
        ((z * NX + x) * NC + k, (((z + dz) % NZ) * NX + (x ^ fx)) * NC + (k ^ fc))
        for z in range(NZ)
        for x in range(NX)
        for k in range(NC)
    ]


def col_perm(dy=0, fh=0):
    return [(y * NH + h, ((y + dy) % NY) * NH + (h ^ fh)) for y in range(NY) for h in range(NH)]


def ring_sides(shard, axis, perm):
    return lax.ppermute(shard, axis, perm(1)), lax.ppermute(shard, axis, perm(-1))


def ring_relay(up, down, axis, perm):
    half = up.shape[0] // 2
    top = lax.ppermute(up[:half], axis, perm(1))
    bottom = lax.ppermute(down[half:], axis, perm(-1))
    return jnp.concatenate([top, bottom], axis=0)


def ring_direct(shard, axis, perm):
    return [shard] + [lax.ppermute(shard, axis, perm(d)) for d in (1, -1, 2)]


def split_bf16(value):
    high = lax.reduce_precision(value, exponent_bits=8, mantissa_bits=7)
    return high.astype(jnp.bfloat16), (value - high).astype(jnp.bfloat16)


def epilogue_kernel(table, running, *refs, inv_snp):
    prods, (row_factor, col_factor, out, values) = refs[:8], refs[8:]
    step = pl.program_id(0)
    row_start = table[32 + step]
    mine = row_factor[...]
    high = mine.astype(jnp.bfloat16)
    low = (mine - high.astype(jnp.float32)).astype(jnp.bfloat16)
    left = jnp.concatenate([high, high, low], axis=1)
    for group in range(8):
        outer = jnp.dot(
            left,
            col_factor[:, group * 256 : (group + 1) * 256],
            preferred_element_type=jnp.float32,
        )
        for side in range(2):
            place = table[48 + group * 2 + side]
            lanes = slice(side * 128, (side + 1) * 128)
            old = running[pl.ds(place, TILE_ROWS, stride=16), :]
            values[pl.ds(place, TILE_ROWS, stride=16), :] = (
                old + prods[group][:, lanes] * inv_snp - outer[:, lanes]
            )

    @pl.when(row_start < NB)
    def _():
        values[...] = jnp.zeros_like(values)

    @pl.when(table[64] == 1)
    def _():
        row_pos = row_start + lax.broadcasted_iota(jnp.int32, (TILE_ROWS, NB), 0)
        lane = lax.broadcasted_iota(jnp.int32, (TILE_ROWS, NB), 1)
        values[pl.ds(0, TILE_ROWS, stride=16), :] = jnp.where(row_pos >= lane, mine, 0.0)

    peak = jnp.full((16, 128), 1e-30, jnp.float32)
    for a in range(TILE_ROWS):
        peak = jnp.maximum(peak, jnp.abs(values[a * 16 : (a + 1) * 16, :]))
    code = jnp.minimum(jnp.ceil(jnp.log(peak) * (1.0 / LOG_STEP)) + 1.0, 8190.0)
    gain = LEVELS / jnp.exp(code * LOG_STEP)
    for a in range(TILE_ROWS):
        scaled = jnp.round(values[a * 16 : (a + 1) * 16, :] * gain)
        out[a * 16 : (a + 1) * 16, :] = scaled.astype(jnp.int32).astype(jnp.int16)
    out[TILE_ROWS * 16 :, :] = code.astype(jnp.int32).astype(jnp.int16)


def epilogue(table, running, prods, row_factor, col_factor, snp_count):
    block = pl.BlockSpec((TILE_ROWS, 256), lambda i, t: (t[16 + i], 0))
    return pl.pallas_call(
        lambda *refs: epilogue_kernel(*refs, inv_snp=1.0 / snp_count),
        grid_spec=pltpu.PrefetchScalarGridSpec(
            num_scalar_prefetch=1,
            grid=(16,),
            in_specs=[
                pl.BlockSpec((TILE_ROWS * 16, 128), lambda i, t: (t[i], 0)),
                *[block] * 8,
                pl.BlockSpec((TILE_ROWS, NB), lambda i, t: (t[16 + i], 0)),
                pl.BlockSpec((3 * NB, 2048), lambda i, t: (0, 0)),
            ],
            out_specs=pl.BlockSpec(((TILE_ROWS + 1) * 16, 128), lambda i, t: (i, 0)),
            scratch_shapes=[pltpu.VMEM((TILE_ROWS * 16, 128), jnp.float32)],
        ),
        out_shape=jax.ShapeDtypeStruct((16 * (TILE_ROWS + 1) * 16, 128), jnp.int16),
        name="epilogue",
    )(table, running, *prods, row_factor, col_factor)


def unpack_kernel(coded, out):
    code = coded[TILE_ROWS * 16 :, :].astype(jnp.float32)
    scale = jnp.exp(code * LOG_STEP) * (1.0 / LEVELS)
    for a in range(TILE_ROWS):
        out[a * 16 : (a + 1) * 16, :] = coded[a * 16 : (a + 1) * 16, :].astype(jnp.float32) * scale


def unpack(coded):
    return pl.pallas_call(
        unpack_kernel,
        grid=(16,),
        in_specs=[pl.BlockSpec(((TILE_ROWS + 1) * 16, 128), lambda i: (i, 0))],
        out_specs=pl.BlockSpec((TILE_ROWS * 16, 128), lambda i: (i, 0)),
        out_shape=jax.ShapeDtypeStruct((16 * TILE_ROWS * 16, 128), jnp.float32),
        name="unpack",
    )(coded)


def on_device(genotypes, running, grid_map):
    row_index = lax.axis_index("row").astype(jnp.uint32)
    col_index = lax.axis_index("col").astype(jnp.uint32)
    z, x_lo, core = row_index >> 2, (row_index >> 1) & 1, row_index & 1
    y, x_hi = col_index >> 1, col_index & 1
    snp_count = genotypes.shape[0]
    inv_snp = 1.0 / snp_count

    def dot0(a, b):
        return lax.dot_general(a, b, (((0,), (0,)), ((), ())), preferred_element_type=jnp.float32)

    across = lax.ppermute(genotypes, "col", col_perm(0, 1))
    y_up, y_down = ring_sides(genotypes, "col", col_perm)
    z_up, z_down = ring_sides(genotypes, "row", row_perm)

    leading = running[:NB, 0, 0, :] + dot0(genotypes, genotypes) * inv_snp
    lower = jnp.linalg.cholesky(leading)
    inverse = lax.linalg.triangular_solve(
        lower, jnp.eye(NB, dtype=jnp.float32), left_side=True, lower=True
    )

    late, across, inverse = lax.optimization_barrier((genotypes, across, inverse))
    beside = lax.ppermute(late, "row", row_perm(0, 1, 0))
    y_opposite = ring_relay(y_up, y_down, "col", col_perm)
    z_opposite = ring_relay(z_up, z_down, "row", row_perm)
    y_up_across, y_down_across = ring_sides(across, "col", col_perm)

    inverse, y_up, z_up = lax.optimization_barrier((inverse, y_up, z_up))
    heard = sum(lax.ppermute(inverse, "row", [(0, d * NX * NC)]) for d in range(1, NZ))
    inverse = jnp.where(z == 0, inverse, heard)
    heard = lax.ppermute(inverse, "row", [(d * NX * NC, d * NX * NC + NC) for d in range(NZ)])
    inverse = jnp.where(x_lo == 0, inverse, heard)
    heard = lax.ppermute(inverse, "row", [(d * NC, d * NC + 1) for d in range(NZ * NX)])
    inverse = jnp.where(core == 0, inverse, heard)

    z_up_side, z_down_side = ring_sides(beside, "row", row_perm)
    y_opposite_across = ring_relay(y_up_across, y_down_across, "col", col_perm)
    z_opposite_side = lax.ppermute(z_opposite, "row", row_perm(0, 1, 0))

    mine_rows = jnp.concatenate(
        [genotypes, across, y_up, y_up_across, y_down, y_down_across, y_opposite, y_opposite_across],
        axis=1,
    )
    col_groups = []
    for own, side in (
        (genotypes, beside),
        (z_up, z_up_side),
        (z_down, z_down_side),
        (z_opposite, z_opposite_side),
    ):
        both = jnp.concatenate([own, side], axis=1)
        col_groups += [both, lax.ppermute(both, "row", row_perm(0, 0, 1))]

    slot0 = jnp.array(SLOT_OF_STEP, jnp.uint32)[(0 - z) & 3]
    lane0 = (x_lo * 128).astype(jnp.int32)
    first = sum(
        jnp.where(
            slot0 * 2 + core == group,
            lax.dynamic_slice_in_dim(g, lane0, 128, 1),
            jnp.zeros((), g.dtype),
        )
        for group, g in enumerate(col_groups)
    )
    panel = dot0(mine_rows, first).reshape(NY * NH, 128, NB)
    panel = jnp.concatenate(
        [panel[2 * SLOT_OF_STEP[b] : 2 * SLOT_OF_STEP[b] + 2] for b in range(NY)], axis=0
    ).reshape(NY * NH * 128, NB)
    panel = running[:, 0, 0, :] + panel * inv_snp
    factor = lax.dot_general(
        panel,
        inverse,
        (((1,), (1,)), ((), ())),
        precision=lax.Precision.HIGHEST,
        preferred_element_type=jnp.float32,
    )
    pieces = factor.reshape(NY, NH, 128, NB)
    heard = lax.ppermute(pieces[:, 1], "col", [(0, 1)])
    pieces = jnp.where(x_hi == 0, pieces[:, 0], heard)
    heard = sum(
        lax.ppermute(pieces[d], "col", [(h, d * NH + h) for h in range(NH)]) for d in range(1, NY)
    )
    own_factor = jnp.where(y == 0, pieces[0], heard)
    pair = jnp.stack([own_factor, lax.ppermute(own_factor, "col", col_perm(0, 1))])
    row_factor = jnp.concatenate(ring_direct(pair, "col", col_perm), axis=0).reshape(1024, NB)
    pair = jnp.stack([own_factor, lax.ppermute(own_factor, "row", row_perm(0, 1, 0))])
    half = jnp.stack(ring_direct(pair, "row", row_perm))
    twin = lax.ppermute(half, "row", row_perm(0, 0, 1))
    high, low = split_bf16(jnp.stack([half, twin], axis=1).reshape(2048, NB).T)
    col_factor = jnp.concatenate([high, low, high], axis=0)

    late_rows, _ = lax.optimization_barrier((mine_rows, factor))
    prods = [dot0(mine_rows if g < 2 else late_rows, col_groups[g]) for g in range(8)]

    tiles = jnp.arange(16, dtype=jnp.uint32)
    hit = grid_map[None, :] == jnp.arange(16, dtype=jnp.int32)[:, None]
    inverse_map = jnp.sum(jnp.where(hit, tiles[None, :], 0), axis=1).astype(jnp.uint32)
    step_y = ((inverse_map >> 2) - y) & 3
    slot = jnp.where(step_y == 0, 0, jnp.where(step_y == 1, 2, jnp.where(step_y == 2, 3, 1)))
    tile = ((slot.astype(jnp.uint32) * 2) + (((inverse_map >> 1) & 1) ^ x_hi)) * 2 + (inverse_map & 1)
    row_start = row_index * 1024 + inverse_map * TILE_ROWS
    slot_z = tiles >> 2
    step_z = jnp.where(slot_z == 0, 0, jnp.where(slot_z == 1, 3, slot_z - 1)).astype(jnp.uint32)
    place = (((step_z + z) & 3) << 2) + (((tiles & 1) ^ x_lo) << 1) + (((tiles >> 1) & 1) ^ core)
    is_col0 = jnp.where(col_index == 0, 1, 0).astype(jnp.uint32)
    table = jnp.concatenate([inverse_map, tile, row_start, place, is_col0[None]]).astype(jnp.int32)

    send = epilogue(table, running.reshape(1024 * 16, 128), prods, row_factor, col_factor, snp_count)
    send = send.reshape(16, (TILE_ROWS + 1) * 16, 128)
    got = lax.all_to_all(send, "row", split_axis=0, concat_axis=0, tiled=True)
    return unpack(got.reshape(-1, 128)).reshape(16, 1, TILE_ROWS, 16, 1, 128)


def solution(mesh):
    in_specs = (P(None, ("row", "col")), P("row", None, "col", None), P())
    out_specs = P(None, "row", None, None, "col", None)
    return jax.shard_map(
        on_device, mesh=mesh, in_specs=in_specs, out_specs=out_specs, check_vma=False
    )
```

```python
import jax
import jax.numpy as jnp
from jax import lax
from jax.experimental import pallas as pl
from jax.experimental.pallas import tpu as pltpu
from jax.sharding import PartitionSpec as P


NB = 128
NZ, NX, NC = 4, 2, 2
NY, NH = 4, 2
SLOT_OF_STEP = (0, 2, 3, 1)
TILE_ROWS = 64
LEVELS = 32767.0
LOG_STEP = 0.6931471805599453 / 64.0


def row_perm(dz=0, fx=0, fc=0):
    return [
        ((z * NX + x) * NC + k, (((z + dz) % NZ) * NX + (x ^ fx)) * NC + (k ^ fc))
        for z in range(NZ)
        for x in range(NX)
        for k in range(NC)
    ]


def col_perm(dy=0, fh=0):
    return [(y * NH + h, ((y + dy) % NY) * NH + (h ^ fh)) for y in range(NY) for h in range(NH)]


def ring_sides(shard, axis, perm):
    return lax.ppermute(shard, axis, perm(1)), lax.ppermute(shard, axis, perm(-1))


def ring_relay(up, down, axis, perm):
    half = up.shape[0] // 2
    top = lax.ppermute(up[:half], axis, perm(1))
    bottom = lax.ppermute(down[half:], axis, perm(-1))
    return jnp.concatenate([top, bottom], axis=0)


def ring_direct(shard, axis, perm):
    return [shard] + [lax.ppermute(shard, axis, perm(d)) for d in (1, -1, 2)]


def split_bf16(value):
    high = lax.reduce_precision(value, exponent_bits=8, mantissa_bits=7)
    return high.astype(jnp.bfloat16), (value - high).astype(jnp.bfloat16)


def epilogue_kernel(table, running, *refs, inv_snp):
    prods, (row_factor, col_factor, out, values) = refs[:4], refs[4:]
    step = pl.program_id(0)
    row_start = table[32 + step]
    mine = row_factor[...]
    high = mine.astype(jnp.bfloat16)
    low = (mine - high.astype(jnp.float32)).astype(jnp.bfloat16)
    left = jnp.concatenate([high, high, low], axis=1)
    for group in range(4):
        outer = jnp.dot(
            left,
            col_factor[:, group * 512 : (group + 1) * 512],
            preferred_element_type=jnp.float32,
        )
        for side in range(4):
            place = table[48 + group * 4 + side]
            lanes = slice(side * 128, (side + 1) * 128)
            old = running[pl.ds(place, TILE_ROWS, stride=16), :]
            values[pl.ds(place, TILE_ROWS, stride=16), :] = (
                old + prods[group][:, lanes] * inv_snp - outer[:, lanes]
            )

    @pl.when(row_start < NB)
    def _():
        values[...] = jnp.zeros_like(values)

    @pl.when(table[64] == 1)
    def _():
        row_pos = row_start + lax.broadcasted_iota(jnp.int32, (TILE_ROWS, NB), 0)
        lane = lax.broadcasted_iota(jnp.int32, (TILE_ROWS, NB), 1)
        values[pl.ds(0, TILE_ROWS, stride=16), :] = jnp.where(row_pos >= lane, mine, 0.0)

    peak = jnp.full((16, 128), 1e-30, jnp.float32)
    for a in range(TILE_ROWS):
        peak = jnp.maximum(peak, jnp.abs(values[a * 16 : (a + 1) * 16, :]))
    code = jnp.minimum(jnp.ceil(jnp.log(peak) * (1.0 / LOG_STEP)) + 1.0, 8190.0)
    gain = LEVELS / jnp.exp(code * LOG_STEP)
    for a in range(TILE_ROWS):
        scaled = jnp.round(values[a * 16 : (a + 1) * 16, :] * gain)
        out[a * 16 : (a + 1) * 16, :] = scaled.astype(jnp.int32).astype(jnp.int16)
    out[TILE_ROWS * 16 :, :] = code.astype(jnp.int32).astype(jnp.int16)


def epilogue(table, running, prods, row_factor, col_factor, snp_count):
    block = pl.BlockSpec((TILE_ROWS, 512), lambda i, t: (t[16 + i], 0))
    return pl.pallas_call(
        lambda *refs: epilogue_kernel(*refs, inv_snp=1.0 / snp_count),
        grid_spec=pltpu.PrefetchScalarGridSpec(
            num_scalar_prefetch=1,
            grid=(16,),
            in_specs=[
                pl.BlockSpec((TILE_ROWS * 16, 128), lambda i, t: (t[i], 0)),
                *[block] * 4,
                pl.BlockSpec((TILE_ROWS, NB), lambda i, t: (t[16 + i], 0)),
                pl.BlockSpec((3 * NB, 2048), lambda i, t: (0, 0)),
            ],
            out_specs=pl.BlockSpec(((TILE_ROWS + 1) * 16, 128), lambda i, t: (i, 0)),
            scratch_shapes=[pltpu.VMEM((TILE_ROWS * 16, 128), jnp.float32)],
        ),
        out_shape=jax.ShapeDtypeStruct((16 * (TILE_ROWS + 1) * 16, 128), jnp.int16),
        name="epilogue",
    )(table, running, *prods, row_factor, col_factor)


K_STEP = 1024


def product_kernel(rows, both, twin, out):
    def add(lanes, part):
        @pl.when(pl.program_id(0) == 0)
        def _():
            out[:, lanes] = part

        @pl.when(pl.program_id(0) > 0)
        def _():
            out[:, lanes] += part

    add(slice(0, 256), jnp.dot(rows[...], both[...], preferred_element_type=jnp.float32))
    add(slice(256, 512), jnp.dot(rows[...], twin[...], preferred_element_type=jnp.float32))


def product(rows, both, twin):
    return pl.pallas_call(
        product_kernel,
        grid=(rows.shape[1] // K_STEP,),
        in_specs=[
            pl.BlockSpec((rows.shape[0], K_STEP), lambda k: (0, k)),
            pl.BlockSpec((K_STEP, 256), lambda k: (k, 0)),
            pl.BlockSpec((K_STEP, 256), lambda k: (k, 0)),
        ],
        out_specs=pl.BlockSpec((rows.shape[0], 512), lambda k: (0, 0)),
        out_shape=jax.ShapeDtypeStruct((rows.shape[0], 512), jnp.float32),
        name="product",
    )(rows, both, twin)


def panel_kernel(pick, rows, old, inverse, *refs, inv_snp):
    groups, (out, first, total, sem) = refs[:8], refs[8:]
    k = pl.program_id(0)

    @pl.when(k == 0)
    def _():
        for g in range(8):
            for f in range(2):

                @pl.when(pick[0] == g * 2 + f)
                def _():
                    copy = pltpu.make_async_copy(
                        groups[g].at[:, f * 128 : (f + 1) * 128], first, sem
                    )
                    copy.start()
                    copy.wait()

        total[...] = jnp.zeros_like(total)

    begin = pl.multiple_of(k * K_STEP, K_STEP)
    total[...] += jnp.dot(
        rows[...], first[pl.ds(begin, K_STEP), :], preferred_element_type=jnp.float32
    )

    @pl.when(k == pl.num_programs(0) - 1)
    def _():
        for b in range(NY * NH):
            rel = 2 * SLOT_OF_STEP[b // NH] + b % NH
            here = slice(b * 128, (b + 1) * 128)
            updated = old[here, :] + total[rel * 128 : (rel + 1) * 128, :] * inv_snp
            out[here, :] = lax.dot_general(
                updated,
                inverse[...],
                (((1,), (1,)), ((), ())),
                precision=lax.Precision.HIGHEST,
                preferred_element_type=jnp.float32,
            )


def panel(pick, rows, old, inverse, groups, snp_count):
    count = rows.shape[0]
    return pl.pallas_call(
        lambda *refs: panel_kernel(*refs, inv_snp=1.0 / snp_count),
        grid_spec=pltpu.PrefetchScalarGridSpec(
            num_scalar_prefetch=1,
            grid=(snp_count // K_STEP,),
            in_specs=[
                pl.BlockSpec((count, K_STEP), lambda k, t: (0, k)),
                pl.BlockSpec((count, NB), lambda k, t: (0, 0)),
                pl.BlockSpec((NB, NB), lambda k, t: (0, 0)),
                *[pl.BlockSpec(memory_space=pl.ANY)] * 8,
            ],
            out_specs=pl.BlockSpec((count, NB), lambda k, t: (0, 0)),
            scratch_shapes=[
                pltpu.VMEM((snp_count, NB), jnp.bfloat16),
                pltpu.VMEM((count, NB), jnp.float32),
                pltpu.SemaphoreType.DMA(()),
            ],
        ),
        out_shape=jax.ShapeDtypeStruct((count, NB), jnp.float32),
        name="panel",
    )(pick, rows, old, inverse, *groups)


def unpack_kernel(coded, out):
    for part in range(2):
        source = part * (TILE_ROWS + 1) * 16
        target = part * TILE_ROWS * 16
        code = coded[source + TILE_ROWS * 16 : source + (TILE_ROWS + 1) * 16, :].astype(jnp.float32)
        scale = jnp.exp(code * LOG_STEP) * (1.0 / LEVELS)
        for a in range(TILE_ROWS):
            values = coded[source + a * 16 : source + (a + 1) * 16, :].astype(jnp.float32)
            out[target + a * 16 : target + (a + 1) * 16, :] = values * scale


def unpack(coded):
    return pl.pallas_call(
        unpack_kernel,
        grid=(8,),
        in_specs=[pl.BlockSpec((2 * (TILE_ROWS + 1) * 16, 128), lambda i: (i, 0))],
        out_specs=pl.BlockSpec((2 * TILE_ROWS * 16, 128), lambda i: (i, 0)),
        out_shape=jax.ShapeDtypeStruct((16 * TILE_ROWS * 16, 128), jnp.float32),
        name="unpack",
    )(coded)


def compute(genotypes, running, grid_map):
    row_index = lax.axis_index("row").astype(jnp.uint32)
    col_index = lax.axis_index("col").astype(jnp.uint32)
    z, x_lo, core = row_index >> 2, (row_index >> 1) & 1, row_index & 1
    y, x_hi = col_index >> 1, col_index & 1
    snp_count = genotypes.shape[0]
    inv_snp = 1.0 / snp_count

    def dot0(a, b):
        return lax.dot_general(a, b, (((0,), (0,)), ((), ())), preferred_element_type=jnp.float32)

    z_up, z_down = ring_sides(genotypes, "row", row_perm)
    turned = genotypes.T
    across = lax.ppermute(turned, "col", col_perm(0, 1))
    y_up, y_down = ring_sides(turned, "col", col_perm)

    leading = running[:NB, 0, 0, :] + dot0(genotypes, genotypes) * inv_snp
    lower = jnp.linalg.cholesky(leading)
    inverse = lax.linalg.triangular_solve(
        lower, jnp.eye(NB, dtype=jnp.float32), left_side=True, lower=True
    )

    late, across, inverse = lax.optimization_barrier((genotypes, across, inverse))
    beside = lax.ppermute(late, "row", row_perm(0, 1, 0))
    y_up_across, y_down_across = ring_sides(across, "col", col_perm)
    z_opposite = ring_relay(z_up, z_down, "row", row_perm)
    y_opposite = ring_relay(y_up, y_down, "col", col_perm)

    inverse, y_up, z_up, z_down, y_down = lax.optimization_barrier(
        (inverse, y_up, z_up, z_down, y_down)
    )
    heard = sum(lax.ppermute(inverse, "row", [(0, d * NX * NC)]) for d in range(1, NZ))
    z_up_side, z_down_side = ring_sides(beside, "row", row_perm)
    z_opposite_side = lax.ppermute(z_opposite, "row", row_perm(0, 1, 0))
    heard, y_up_across, y_down_across = lax.optimization_barrier(
        (heard, y_up_across, y_down_across)
    )
    y_opposite_across = ring_relay(y_up_across, y_down_across, "col", col_perm)
    inverse = jnp.where(z == 0, inverse, heard)
    heard = lax.ppermute(inverse, "row", [(d * NX * NC, d * NX * NC + NC) for d in range(NZ)])
    heard, z_up_side, z_down_side = lax.optimization_barrier((heard, z_up_side, z_down_side))
    inverse = jnp.where(x_lo == 0, inverse, heard)
    heard = lax.ppermute(inverse, "row", [(d * NC, d * NC + 1) for d in range(NZ * NX)])
    inverse = jnp.where(core == 0, inverse, heard)

    mine_rows = jnp.concatenate(
        [turned, across, y_up, y_up_across, y_down, y_down_across, y_opposite, y_opposite_across],
        axis=0,
    )
    col_groups = []
    for own, side in (
        (genotypes, beside),
        (z_up, z_up_side),
        (z_down, z_down_side),
        (z_opposite, z_opposite_side),
    ):
        both = jnp.concatenate([own, side], axis=1)
        col_groups += [both, lax.ppermute(both, "row", row_perm(0, 0, 1))]

    away = (0 - z) & 3
    slot0 = jnp.where(away == 0, 0, jnp.where(away == 1, 2, jnp.where(away == 2, 3, 1)))
    pick = ((slot0.astype(jnp.uint32) * 2 + core) * 2 + x_lo).astype(jnp.int32)[None]
    factor = panel(pick, mine_rows, running[:, 0, 0, :], inverse, col_groups, snp_count)
    pieces = factor.reshape(NY, NH, 128, NB)
    heard = lax.ppermute(pieces[:, 1], "col", [(0, 1)])
    pieces = jnp.where(x_hi == 0, pieces[:, 0], heard)
    heard = sum(
        lax.ppermute(pieces[d], "col", [(h, d * NH + h) for h in range(NH)]) for d in range(1, NY)
    )
    own_factor = jnp.where(y == 0, pieces[0], heard)
    pair = jnp.stack([own_factor, lax.ppermute(own_factor, "col", col_perm(0, 1))])
    row_factor = jnp.concatenate(ring_direct(pair, "col", col_perm), axis=0).reshape(1024, NB)
    pair = jnp.stack([own_factor, lax.ppermute(own_factor, "row", row_perm(0, 1, 0))])
    half = jnp.stack(ring_direct(pair, "row", row_perm))
    twin = lax.ppermute(half, "row", row_perm(0, 0, 1))
    high, low = split_bf16(jnp.stack([half, twin], axis=1).reshape(2048, NB).T)
    col_factor = jnp.concatenate([high, low, high], axis=0)

    late_rows, _ = lax.optimization_barrier((mine_rows, factor))
    prods = []
    for g in range(4):
        prods.append(product(late_rows, col_groups[2 * g], col_groups[2 * g + 1]))

    tiles = jnp.arange(16, dtype=jnp.uint32)
    hit = grid_map[None, :] == jnp.arange(16, dtype=jnp.int32)[:, None]
    inverse_map = jnp.sum(jnp.where(hit, tiles[None, :], 0), axis=1).astype(jnp.uint32)
    step_y = ((inverse_map >> 2) - y) & 3
    slot = jnp.where(step_y == 0, 0, jnp.where(step_y == 1, 2, jnp.where(step_y == 2, 3, 1)))
    tile = ((slot.astype(jnp.uint32) * 2) + (((inverse_map >> 1) & 1) ^ x_hi)) * 2 + (inverse_map & 1)
    row_start = row_index * 1024 + inverse_map * TILE_ROWS
    slot_z = tiles >> 2
    step_z = jnp.where(slot_z == 0, 0, jnp.where(slot_z == 1, 3, slot_z - 1)).astype(jnp.uint32)
    place = (((step_z + z) & 3) << 2) + (((tiles & 1) ^ x_lo) << 1) + (((tiles >> 1) & 1) ^ core)
    is_col0 = jnp.where(col_index == 0, 1, 0).astype(jnp.uint32)
    table = jnp.concatenate([inverse_map, tile, row_start, place, is_col0[None]]).astype(jnp.int32)

    packed = epilogue(table, running.reshape(1024 * 16, 128), prods, row_factor, col_factor, snp_count)
    packed = packed.reshape(16, (TILE_ROWS + 1) * 16, 128)
    got = lax.all_to_all(packed, "row", split_axis=0, concat_axis=0, tiled=True)
    return unpack(got.reshape(-1, 128)).reshape(16, 1, TILE_ROWS, 16, 1, 128)


def solution(mesh):
    in_specs = (P(None, ("row", "col")), P("row", None, "col", None), P())
    out_specs = P(None, "row", None, None, "col", None)
    return jax.shard_map(
        compute, mesh=mesh, in_specs=in_specs, out_specs=out_specs, check_vma=False
    )
```

```python
import jax
import jax.numpy as jnp
from jax import lax
from jax.experimental import pallas as pl
from jax.experimental.pallas import tpu as pltpu
from jax.sharding import PartitionSpec as P


NB = 128
NZ, NX, NC = 4, 2, 2
NY, NH = 4, 2
STEP_OF_SLOT = (0, 3, 1, 2)
HALVES = 2
TILE_ROWS = 64 // HALVES
LEVELS = 32767.0
LOG_STEP = 0.6931471805599453 / 64.0


def row_perm(dz=0, fx=0, fc=0):
    return [
        ((z * NX + x) * NC + k, (((z + dz) % NZ) * NX + (x ^ fx)) * NC + (k ^ fc))
        for z in range(NZ)
        for x in range(NX)
        for k in range(NC)
    ]


def col_perm(dy=0, fh=0):
    return [(y * NH + h, ((y + dy) % NY) * NH + (h ^ fh)) for y in range(NY) for h in range(NH)]


def ring_sides(shard, axis, perm):
    return lax.ppermute(shard, axis, perm(1)), lax.ppermute(shard, axis, perm(-1))


def ring_relay(up, down, axis, perm):
    half = up.shape[0] // 2
    top = lax.ppermute(up[:half], axis, perm(1))
    bottom = lax.ppermute(down[half:], axis, perm(-1))
    return top, bottom


def ring_direct(shard, axis, perm):
    return [shard] + [lax.ppermute(shard, axis, perm(d)) for d in (1, -1, 2)]


def split_bf16(value):
    high = lax.reduce_precision(value, exponent_bits=8, mantissa_bits=7)
    return high.astype(jnp.bfloat16), (value - high).astype(jnp.bfloat16)


def epilogue_kernel(table, running, *refs, part, inv_snp):
    prods, (row_factor, col_factor, out, values) = refs[:4], refs[4:]
    step = pl.program_id(0)
    row_start = table[32 + step] + part * TILE_ROWS
    mine = row_factor[...]
    high = mine.astype(jnp.bfloat16)
    low = (mine - high.astype(jnp.float32)).astype(jnp.bfloat16)
    left = jnp.concatenate([high, high, low], axis=1)
    for group in range(4):
        outer = jnp.dot(
            left,
            col_factor[:, group * 512 : (group + 1) * 512],
            preferred_element_type=jnp.float32,
        )
        for side in range(4):
            place = table[48 + group * 4 + side]
            lanes = slice(side * 128, (side + 1) * 128)
            old = running[pl.ds(place, TILE_ROWS, stride=16), :]
            values[pl.ds(place, TILE_ROWS, stride=16), :] = (
                old + prods[group][:, lanes] * inv_snp - outer[:, lanes]
            )

    @pl.when(row_start < NB)
    def _():
        values[...] = jnp.zeros_like(values)

    @pl.when(table[64] == 1)
    def _():
        row_pos = row_start + lax.broadcasted_iota(jnp.int32, (TILE_ROWS, NB), 0)
        lane = lax.broadcasted_iota(jnp.int32, (TILE_ROWS, NB), 1)
        values[pl.ds(0, TILE_ROWS, stride=16), :] = jnp.where(row_pos >= lane, mine, 0.0)

    peak = jnp.full((16, 128), 1e-30, jnp.float32)
    for a in range(TILE_ROWS):
        peak = jnp.maximum(peak, jnp.abs(values[a * 16 : (a + 1) * 16, :]))
    code = jnp.minimum(jnp.ceil(jnp.log(peak) * (1.0 / LOG_STEP)) + 1.0, 8190.0)
    gain = LEVELS / jnp.exp(code * LOG_STEP)
    for a in range(TILE_ROWS):
        scaled = jnp.round(values[a * 16 : (a + 1) * 16, :] * gain)
        out[a * 16 : (a + 1) * 16, :] = scaled.astype(jnp.int32).astype(jnp.int16)
    out[TILE_ROWS * 16 :, :] = code.astype(jnp.int32).astype(jnp.int16)


def epilogue(part, table, running, prods, row_factor, col_factor, snp_count):
    block = pl.BlockSpec((TILE_ROWS, 512), lambda i, t: (t[16 + i] * HALVES + part, 0))
    return pl.pallas_call(
        lambda *refs: epilogue_kernel(*refs, part=part, inv_snp=1.0 / snp_count),
        grid_spec=pltpu.PrefetchScalarGridSpec(
            num_scalar_prefetch=1,
            grid=(16,),
            in_specs=[
                pl.BlockSpec((TILE_ROWS * 16, 128), lambda i, t: (t[i] * HALVES + part, 0)),
                *[block] * 4,
                pl.BlockSpec((TILE_ROWS, NB), lambda i, t: (t[16 + i] * HALVES + part, 0)),
                pl.BlockSpec((3 * NB, 2048), lambda i, t: (0, 0)),
            ],
            out_specs=pl.BlockSpec(((TILE_ROWS + 1) * 16, 128), lambda i, t: (i, 0)),
            scratch_shapes=[pltpu.VMEM((TILE_ROWS * 16, 128), jnp.float32)],
        ),
        out_shape=jax.ShapeDtypeStruct((16 * (TILE_ROWS + 1) * 16, 128), jnp.int16),
        name="epilogue",
    )(table, running, *prods, row_factor, col_factor)


ROW_STEP = 256
ROW_PLACES = ((0, 0, 0), (0, 1, 128), (1, 2, 0), (1, 3, 128), (2, 4, 0), (2, 5, 128))
ROW_PLACES += ((3, 6, 0), (3, 7, 64), (3, 8, 128), (3, 9, 192))


def fetch_rows(parts, rows, sems, others=()):
    step = pl.program_id(0)

    def copies(n):
        places = [(part, row) for where, part, row in ROW_PLACES if where == n]
        return [
            pltpu.make_async_copy(
                parts[part],
                rows.at[n % 2, row : row + parts[part].shape[0], :],
                sems.at[n % 2, number],
            )
            for number, (part, row) in enumerate(places)
        ]

    for n in range(4):

        @pl.when(step == n)
        def _():
            if n == 0:
                for copy in list(others) + copies(0):
                    copy.start()
            if n < 3:
                for copy in copies(n + 1):
                    copy.start()
            for copy in copies(n) + (list(others) if n == 0 else []):
                copy.wait()


def product_kernel(*refs):
    parts, shards, (out, rows, cols, row_sems, col_sems) = refs[:10], refs[10:14], refs[14:]
    others = [
        pltpu.make_async_copy(
            shards[n], cols.at[:, n * 128 : (n + 1) * 128], col_sems.at[n]
        )
        for n in range(4)
    ]
    fetch_rows(parts, rows, row_sems, others)
    out[...] = jnp.dot(
        rows[pl.program_id(0) % 2], cols[...], preferred_element_type=jnp.float32
    )


def product(parts, shards):
    count = shards[0].shape[0]
    return pl.pallas_call(
        product_kernel,
        grid=(4,),
        in_specs=[pl.BlockSpec(memory_space=pl.ANY)] * 14,
        out_specs=pl.BlockSpec((ROW_STEP, 512), lambda i: (i, 0)),
        scratch_shapes=[
            pltpu.VMEM((2, ROW_STEP, count), jnp.bfloat16),
            pltpu.VMEM((count, 512), jnp.bfloat16),
            pltpu.SemaphoreType.DMA((2, 4)),
            pltpu.SemaphoreType.DMA((4,)),
        ],
        out_shape=jax.ShapeDtypeStruct((4 * ROW_STEP, 512), jnp.float32),
        name="product",
    )(*parts, *shards)


def panel_kernel(pick, old, inverse, *refs, inv_snp):
    parts, shards, (out, rows, first, row_sems, sem) = refs[:10], refs[10:26], refs[26:]

    @pl.when(pl.program_id(0) == 0)
    def _():
        for n in range(16):

            @pl.when(pick[0] == n)
            def _():
                copy = pltpu.make_async_copy(shards[n], first, sem)
                copy.start()
                copy.wait()

    fetch_rows(parts, rows, row_sems)
    product_rows = jnp.dot(
        rows[pl.program_id(0) % 2], first[...], preferred_element_type=jnp.float32
    )
    out[...] = lax.dot_general(
        old[...] + product_rows * inv_snp,
        inverse[...],
        (((1,), (1,)), ((), ())),
        precision=lax.Precision.HIGHEST,
        preferred_element_type=jnp.float32,
    )


def panel(pick, old, inverse, parts, shards):
    count = shards[0].shape[0]
    block = pl.BlockSpec((ROW_STEP, NB), lambda i, t: (t[1 + i], 0))
    return pl.pallas_call(
        lambda *refs: panel_kernel(*refs, inv_snp=1.0 / count),
        grid_spec=pltpu.PrefetchScalarGridSpec(
            num_scalar_prefetch=1,
            grid=(4,),
            in_specs=[
                block,
                pl.BlockSpec((NB, NB), lambda i, t: (0, 0)),
                *[pl.BlockSpec(memory_space=pl.ANY)] * 26,
            ],
            out_specs=block,
            scratch_shapes=[
                pltpu.VMEM((2, ROW_STEP, count), jnp.bfloat16),
                pltpu.VMEM((count, NB), jnp.bfloat16),
                pltpu.SemaphoreType.DMA((2, 4)),
                pltpu.SemaphoreType.DMA(()),
            ],
        ),
        out_shape=jax.ShapeDtypeStruct((4 * ROW_STEP, NB), jnp.float32),
        name="panel",
    )(pick, old, inverse, *parts, *shards)


def unpack_kernel(coded, *refs):
    out = refs[-1]
    for source in range(2):
        code = coded[source, TILE_ROWS * 16 :, :].astype(jnp.float32)
        scale = jnp.exp(code * LOG_STEP) * (1.0 / LEVELS)
        for a in range(TILE_ROWS):
            values = coded[source, a * 16 : (a + 1) * 16, :].astype(jnp.float32)
            out[source, 0, a * 16 : (a + 1) * 16, :] = values * scale


def unpack(part, coded, before):
    begun = [] if before is None else [before]
    return pl.pallas_call(
        unpack_kernel,
        grid=(8,),
        in_specs=[
            pl.BlockSpec((2, (TILE_ROWS + 1) * 16, 128), lambda i: (i, 0, 0)),
            *[pl.BlockSpec(memory_space=pl.ANY)] * len(begun),
        ],
        out_specs=pl.BlockSpec((2, 1, TILE_ROWS * 16, 128), lambda i: (i, part, 0, 0)),
        out_shape=jax.ShapeDtypeStruct((16, HALVES, TILE_ROWS * 16, 128), jnp.float32),
        input_output_aliases={1: 0} if begun else {},
        name="unpack",
    )(coded, *begun)


def compute(genotypes, running, grid_map):
    row_index = lax.axis_index("row").astype(jnp.uint32)
    col_index = lax.axis_index("col").astype(jnp.uint32)
    z, x_lo, core = row_index >> 2, (row_index >> 1) & 1, row_index & 1
    y, x_hi = col_index >> 1, col_index & 1
    snp_count = genotypes.shape[0]
    inv_snp = 1.0 / snp_count

    def dot0(a, b):
        return lax.dot_general(a, b, (((0,), (0,)), ((), ())), preferred_element_type=jnp.float32)

    def twin(value):
        return lax.ppermute(value, "row", row_perm(0, 0, 1))

    z_up, z_down = ring_sides(genotypes, "row", row_perm)
    turned = genotypes.T
    across = lax.ppermute(turned, "col", col_perm(0, 1))
    y_up, y_down = ring_sides(turned, "col", col_perm)
    own_twin = twin(genotypes)

    leading = running[:NB, 0, 0, :] + dot0(genotypes, genotypes) * inv_snp
    lower = jnp.linalg.cholesky(leading)

    late, across, lower = lax.optimization_barrier((genotypes, across, lower))
    beside = lax.ppermute(late, "row", row_perm(0, 1, 0))
    y_up_across, y_down_across = ring_sides(across, "col", col_perm)
    z_opposite = jnp.concatenate(ring_relay(z_up, z_down, "row", row_perm), axis=0)
    y_opposite = ring_relay(y_up, y_down, "col", col_perm)
    z_up_twin, z_down_twin = twin(z_up), twin(z_down)
    inverse = lax.linalg.triangular_solve(
        lower, jnp.eye(NB, dtype=jnp.float32), left_side=True, lower=True
    )

    heard = sum(lax.ppermute(inverse, "row", [(0, d * NX * NC)]) for d in range(1, NZ))
    inverse = jnp.where(z == 0, inverse, heard)
    z_up_side, z_down_side = ring_sides(beside, "row", row_perm)
    heard = lax.ppermute(inverse, "row", [(d * NX * NC, d * NX * NC + NC) for d in range(NZ)])
    inverse = jnp.where(x_lo == 0, inverse, heard)
    z_opposite_side = lax.ppermute(z_opposite, "row", row_perm(0, 1, 0))
    y_opposite_across = ring_relay(y_up_across, y_down_across, "col", col_perm)
    heard = lax.ppermute(inverse, "row", [(d * NC, d * NC + 1) for d in range(NZ * NX)])
    inverse = jnp.where(core == 0, inverse, heard)

    row_parts = [turned, across, y_up, y_up_across, y_down, y_down_across]
    row_parts += [*y_opposite, *y_opposite_across]
    col_shards = [
        (genotypes, beside, own_twin, twin(beside)),
        (z_up, z_up_side, z_up_twin, twin(z_up_side)),
        (z_down, z_down_side, z_down_twin, twin(z_down_side)),
        (z_opposite, z_opposite_side, twin(z_opposite), twin(z_opposite_side)),
    ]

    away = (0 - z) & 3
    slot0 = jnp.where(away == 0, 0, jnp.where(away == 1, 2, jnp.where(away == 2, 3, 1)))
    pick = ((slot0.astype(jnp.uint32) * 2 + core) * 2 + x_lo).astype(jnp.int32)
    pick = jnp.stack([pick, *[jnp.int32(step) for step in STEP_OF_SLOT]])
    factor = panel(
        pick, running[:, 0, 0, :], inverse, row_parts, [s for group in col_shards for s in group]
    )
    pieces = factor.reshape(NY, NH, 128, NB)
    heard = lax.ppermute(pieces[:, 1], "col", [(0, 1)])
    pieces = jnp.where(x_hi == 0, pieces[:, 0], heard)
    heard = sum(
        lax.ppermute(pieces[d], "col", [(h, d * NH + h) for h in range(NH)]) for d in range(1, NY)
    )
    own_factor = jnp.where(y == 0, pieces[0], heard)
    pair = jnp.stack([own_factor, lax.ppermute(own_factor, "col", col_perm(0, 1))])
    row_factor = jnp.concatenate(ring_direct(pair, "col", col_perm), axis=0).reshape(1024, NB)
    pair = jnp.stack([own_factor, lax.ppermute(own_factor, "row", row_perm(0, 1, 0))])
    half = jnp.stack(ring_direct(pair, "row", row_perm))
    half_twin = lax.ppermute(half, "row", row_perm(0, 0, 1))
    high, low = split_bf16(jnp.stack([half, half_twin], axis=1).reshape(2048, NB).T)
    col_factor = jnp.concatenate([high, low, high], axis=0)

    late_rows, _ = lax.optimization_barrier((row_parts, factor))
    prods = []
    for g in range(4):
        prods.append(product(late_rows, col_shards[g]))

    tiles = jnp.arange(16, dtype=jnp.uint32)
    hit = grid_map[None, :] == jnp.arange(16, dtype=jnp.int32)[:, None]
    inverse_map = jnp.sum(jnp.where(hit, tiles[None, :], 0), axis=1).astype(jnp.uint32)
    step_y = ((inverse_map >> 2) - y) & 3
    slot = jnp.where(step_y == 0, 0, jnp.where(step_y == 1, 2, jnp.where(step_y == 2, 3, 1)))
    tile = ((slot.astype(jnp.uint32) * 2) + (((inverse_map >> 1) & 1) ^ x_hi)) * 2 + (inverse_map & 1)
    row_start = row_index * 1024 + inverse_map * 64
    slot_z = tiles >> 2
    step_z = jnp.where(slot_z == 0, 0, jnp.where(slot_z == 1, 3, slot_z - 1)).astype(jnp.uint32)
    place = (((step_z + z) & 3) << 2) + (((tiles & 1) ^ x_lo) << 1) + (((tiles >> 1) & 1) ^ core)
    is_col0 = jnp.where(col_index == 0, 1, 0).astype(jnp.uint32)
    table = jnp.concatenate([inverse_map, tile, row_start, place, is_col0[None]]).astype(jnp.int32)

    result = None
    running = running.reshape(1024 * 16, 128)
    for part in range(HALVES):
        packed = epilogue(part, table, running, prods, row_factor, col_factor, snp_count)
        packed = packed.reshape(16, (TILE_ROWS + 1) * 16, 128)
        coded = lax.all_to_all(packed, "row", split_axis=0, concat_axis=0, tiled=True)
        result = unpack(part, coded, result)
    return result.reshape(16, 1, 64, 16, 1, 128)


def solution(mesh):
    in_specs = (P(None, ("row", "col")), P("row", None, "col", None), P())
    out_specs = P(None, "row", None, None, "col", None)
    return jax.shard_map(
        compute, mesh=mesh, in_specs=in_specs, out_specs=out_specs, check_vma=False
    )
```

```python
import jax
import jax.numpy as jnp
from jax import lax
from jax.experimental import pallas as pl
from jax.experimental.pallas import tpu as pltpu
from jax.sharding import PartitionSpec as P


NB = 128
NZ, NX, NC = 4, 2, 2
NY, NH = 4, 2
STEP_OF_SLOT = (0, 3, 1, 2)
TILE_ROWS = 64
HALF = 8
PAIRS = TILE_ROWS * HALF // 16
CODED_ROWS = TILE_ROWS * HALF + 16
LEVELS = 32767.0
LOG_STEP = 0.6931471805599453 / 64.0


def row_perm(dz=0, fx=0, fc=0):
    return [
        ((z * NX + x) * NC + k, (((z + dz) % NZ) * NX + (x ^ fx)) * NC + (k ^ fc))
        for z in range(NZ)
        for x in range(NX)
        for k in range(NC)
    ]


def col_perm(dy=0, fh=0):
    return [(y * NH + h, ((y + dy) % NY) * NH + (h ^ fh)) for y in range(NY) for h in range(NH)]


def ring_sides(shard, axis, perm):
    return lax.ppermute(shard, axis, perm(1)), lax.ppermute(shard, axis, perm(-1))


def ring_relay(up, down, axis, perm):
    half = up.shape[0] // 2
    top = lax.ppermute(up[:half], axis, perm(1))
    bottom = lax.ppermute(down[half:], axis, perm(-1))
    return top, bottom


def ring_direct(shard, axis, perm):
    return [shard] + [lax.ppermute(shard, axis, perm(d)) for d in (1, -1, 2)]


def split_bf16(value):
    high = lax.reduce_precision(value, exponent_bits=8, mantissa_bits=7)
    return high.astype(jnp.bfloat16), (value - high).astype(jnp.bfloat16)


def epilogue_kernel(table, running, *refs, part, inv_snp):
    prods, col_factors, (row_factor, out, values) = refs[:2], refs[2:4], refs[4:]
    step = pl.program_id(0)
    row_start = table[32 + step]
    old_rows = running.reshape(TILE_ROWS * HALF, 128)
    mine = row_factor[...]
    high = mine.astype(jnp.bfloat16)
    low = (mine - high.astype(jnp.float32)).astype(jnp.bfloat16)
    left = jnp.concatenate([high, high, low], axis=1)
    for plane in range(2):
        outer = jnp.dot(left, col_factors[plane][...], preferred_element_type=jnp.float32)
        for side in range(4):
            place = table[48 + side] + plane * 4
            lanes = slice(side * 128, (side + 1) * 128)
            old = old_rows[pl.ds(place, TILE_ROWS, stride=HALF), :]
            values[pl.ds(place, TILE_ROWS, stride=HALF), :] = (
                old + prods[plane][:, lanes] * inv_snp - outer[:, lanes]
            )

    @pl.when(row_start < NB)
    def _():
        values[...] = jnp.zeros_like(values)

    if part == 0:

        @pl.when(table[56] == 1)
        def _():
            row_pos = row_start + lax.broadcasted_iota(jnp.int32, (TILE_ROWS, NB), 0)
            lane = lax.broadcasted_iota(jnp.int32, (TILE_ROWS, NB), 1)
            values[pl.ds(0, TILE_ROWS, stride=HALF), :] = jnp.where(row_pos >= lane, mine, 0.0)

    peak = jnp.full((16, 128), 1e-30, jnp.float32)
    for a in range(PAIRS):
        peak = jnp.maximum(peak, jnp.abs(values[a * 16 : (a + 1) * 16, :]))
    peak = jnp.maximum(peak[:8], peak[8:])
    code = jnp.minimum(jnp.ceil(jnp.log(peak) * (1.0 / LOG_STEP)) + 1.0, 8190.0)
    code = jnp.concatenate([code, code], axis=0)
    gain = LEVELS / jnp.exp(code * LOG_STEP)
    for a in range(PAIRS):
        scaled = jnp.round(values[a * 16 : (a + 1) * 16, :] * gain)
        out[a * 16 : (a + 1) * 16, :] = scaled.astype(jnp.int32).astype(jnp.int16)
    out[TILE_ROWS * HALF :, :] = code.astype(jnp.int32).astype(jnp.int16)


def epilogue(part, table, running, prods, row_factor, col_factor, snp_count):
    block = pl.BlockSpec((TILE_ROWS, 512), lambda i, t: (t[16 + i], 0))
    return pl.pallas_call(
        lambda *refs: epilogue_kernel(*refs, part=part, inv_snp=1.0 / snp_count),
        grid_spec=pltpu.PrefetchScalarGridSpec(
            num_scalar_prefetch=1,
            grid=(16,),
            in_specs=[
                pl.BlockSpec((TILE_ROWS, HALF, 128), lambda i, t: (t[i], part, 0)),
                block,
                block,
                pl.BlockSpec((3 * NB, 512), lambda i, t: (0, t[52 + part * 2])),
                pl.BlockSpec((3 * NB, 512), lambda i, t: (0, t[53 + part * 2])),
                pl.BlockSpec((TILE_ROWS, NB), lambda i, t: (t[16 + i], 0)),
            ],
            out_specs=pl.BlockSpec((CODED_ROWS, 128), lambda i, t: (i, 0)),
            scratch_shapes=[pltpu.VMEM((TILE_ROWS * HALF, 128), jnp.float32)],
        ),
        out_shape=jax.ShapeDtypeStruct((16 * CODED_ROWS, 128), jnp.int16),
        name="epilogue",
    )(table, running, *prods, col_factor, col_factor, row_factor)


ROW_STEP = 256
ROW_PLACES = ((0, 0, 0), (0, 1, 128), (1, 2, 0), (1, 3, 128), (2, 4, 0), (2, 5, 128))
ROW_PLACES += ((3, 6, 0), (3, 7, 64), (3, 8, 128), (3, 9, 192))


def fetch_rows(parts, rows, sems):
    step = pl.program_id(0)

    def copies(n):
        places = [(part, row) for where, part, row in ROW_PLACES if where == n]
        return [
            pltpu.make_async_copy(
                parts[part],
                rows.at[n % 2, row : row + parts[part].shape[0], :],
                sems.at[n % 2, number],
            )
            for number, (part, row) in enumerate(places)
        ]

    for n in range(4):

        @pl.when(step == n)
        def _():
            if n == 0:
                for copy in copies(0):
                    copy.start()
            if n < 3:
                for copy in copies(n + 1):
                    copy.start()
            for copy in copies(n):
                copy.wait()


def product_kernel(slots, *refs, plane):
    parts, shards, (out, rows, cols, row_sems, col_sems) = refs[:10], refs[10:26], refs[26:]
    first = pl.program_id(0) == 0

    def copy(slot, side):
        return pltpu.make_async_copy(
            shards[slot * 4 + side], cols.at[:, side * 128 : (side + 1) * 128], col_sems.at[side]
        )

    for slot in range(4):

        @pl.when(jnp.logical_and(first, slots[plane] == slot))
        def _():
            for side in range(4):
                copy(slot, side).start()

    fetch_rows(parts, rows, row_sems)

    @pl.when(first)
    def _():
        for side in range(4):
            copy(0, side).wait()

    out[...] = jnp.dot(
        rows[pl.program_id(0) % 2], cols[...], preferred_element_type=jnp.float32
    )


def product(plane, slots, parts, shards):
    count = shards[0].shape[0]
    return pl.pallas_call(
        lambda *refs: product_kernel(*refs, plane=plane),
        grid_spec=pltpu.PrefetchScalarGridSpec(
            num_scalar_prefetch=1,
            grid=(4,),
            in_specs=[pl.BlockSpec(memory_space=pl.ANY)] * 26,
            out_specs=pl.BlockSpec((ROW_STEP, 512), lambda i, t: (i, 0)),
            scratch_shapes=[
                pltpu.VMEM((2, ROW_STEP, count), jnp.bfloat16),
                pltpu.VMEM((count, 512), jnp.bfloat16),
                pltpu.SemaphoreType.DMA((2, 4)),
                pltpu.SemaphoreType.DMA((4,)),
            ],
        ),
        out_shape=jax.ShapeDtypeStruct((4 * ROW_STEP, 512), jnp.float32),
        name="product",
    )(slots, *parts, *shards)


def panel_kernel(pick, old, inverse, *refs, inv_snp):
    parts, shards, (out, rows, first, row_sems, sem) = refs[:10], refs[10:26], refs[26:]

    @pl.when(pl.program_id(0) == 0)
    def _():
        for n in range(16):

            @pl.when(pick[0] == n)
            def _():
                copy = pltpu.make_async_copy(shards[n], first, sem)
                copy.start()
                copy.wait()

    fetch_rows(parts, rows, row_sems)
    product_rows = jnp.dot(
        rows[pl.program_id(0) % 2], first[...], preferred_element_type=jnp.float32
    )
    out[...] = lax.dot_general(
        old[...] + product_rows * inv_snp,
        inverse[...],
        (((1,), (1,)), ((), ())),
        precision=lax.Precision.HIGHEST,
        preferred_element_type=jnp.float32,
    )


def panel(pick, old, inverse, parts, shards):
    count = shards[0].shape[0]
    block = pl.BlockSpec((ROW_STEP, NB), lambda i, t: (t[1 + i], 0))
    return pl.pallas_call(
        lambda *refs: panel_kernel(*refs, inv_snp=1.0 / count),
        grid_spec=pltpu.PrefetchScalarGridSpec(
            num_scalar_prefetch=1,
            grid=(4,),
            in_specs=[
                block,
                pl.BlockSpec((NB, NB), lambda i, t: (0, 0)),
                *[pl.BlockSpec(memory_space=pl.ANY)] * 26,
            ],
            out_specs=block,
            scratch_shapes=[
                pltpu.VMEM((2, ROW_STEP, count), jnp.bfloat16),
                pltpu.VMEM((count, NB), jnp.bfloat16),
                pltpu.SemaphoreType.DMA((2, 4)),
                pltpu.SemaphoreType.DMA(()),
            ],
        ),
        out_shape=jax.ShapeDtypeStruct((4 * ROW_STEP, NB), jnp.float32),
        name="panel",
    )(pick, old, inverse, *parts, *shards)


def unpack_kernel(coded, *refs):
    out = refs[-1]
    for source in range(2):
        code = coded[source, TILE_ROWS * HALF :, :].astype(jnp.float32)
        scale = jnp.exp(code * LOG_STEP) * (1.0 / LEVELS)
        for a in range(PAIRS):
            values = coded[source, a * 16 : (a + 1) * 16, :].astype(jnp.float32) * scale
            row = source * TILE_ROWS + a * 2
            out[row : row + 2] = values.reshape(2, HALF, 128)


def unpack(part, coded, before):
    begun = [] if before is None else [before]
    return pl.pallas_call(
        unpack_kernel,
        grid=(8,),
        in_specs=[
            pl.BlockSpec((2, CODED_ROWS, 128), lambda i: (i, 0, 0)),
            *[pl.BlockSpec(memory_space=pl.ANY)] * len(begun),
        ],
        out_specs=pl.BlockSpec((2 * TILE_ROWS, HALF, 128), lambda i: (i, part, 0)),
        out_shape=jax.ShapeDtypeStruct((16 * TILE_ROWS, 2 * HALF, 128), jnp.float32),
        input_output_aliases={1: 0} if begun else {},
        name="unpack",
    )(coded, *begun)


def compute(genotypes, running, grid_map):
    row_index = lax.axis_index("row").astype(jnp.uint32)
    col_index = lax.axis_index("col").astype(jnp.uint32)
    z, x_lo, core = row_index >> 2, (row_index >> 1) & 1, row_index & 1
    y, x_hi = col_index >> 1, col_index & 1
    snp_count = genotypes.shape[0]
    inv_snp = 1.0 / snp_count

    def dot0(a, b):
        return lax.dot_general(a, b, (((0,), (0,)), ((), ())), preferred_element_type=jnp.float32)

    def twin(value):
        return lax.ppermute(value, "row", row_perm(0, 0, 1))

    z_up, z_down = ring_sides(genotypes, "row", row_perm)
    turned = genotypes.T
    across = lax.ppermute(turned, "col", col_perm(0, 1))
    y_up, y_down = ring_sides(turned, "col", col_perm)
    own_twin = twin(genotypes)

    leading = running[:NB, 0, 0, :] + dot0(genotypes, genotypes) * inv_snp
    lower = jnp.linalg.cholesky(leading)

    late, across, lower = lax.optimization_barrier((genotypes, across, lower))
    beside = lax.ppermute(late, "row", row_perm(0, 1, 0))
    y_up_across, y_down_across = ring_sides(across, "col", col_perm)
    z_opposite = jnp.concatenate(ring_relay(z_up, z_down, "row", row_perm), axis=0)
    y_opposite = ring_relay(y_up, y_down, "col", col_perm)
    z_up_twin, z_down_twin = twin(z_up), twin(z_down)
    inverse = lax.linalg.triangular_solve(
        lower, jnp.eye(NB, dtype=jnp.float32), left_side=True, lower=True
    )

    heard = sum(lax.ppermute(inverse, "row", [(0, d * NX * NC)]) for d in range(1, NZ))
    inverse = jnp.where(z == 0, inverse, heard)
    z_up_side, z_down_side = ring_sides(beside, "row", row_perm)
    heard = lax.ppermute(inverse, "row", [(d * NX * NC, d * NX * NC + NC) for d in range(NZ)])
    inverse = jnp.where(x_lo == 0, inverse, heard)
    z_opposite_side = lax.ppermute(z_opposite, "row", row_perm(0, 1, 0))
    y_opposite_across = ring_relay(y_up_across, y_down_across, "col", col_perm)
    heard = lax.ppermute(inverse, "row", [(d * NC, d * NC + 1) for d in range(NZ * NX)])
    inverse = jnp.where(core == 0, inverse, heard)

    row_parts = [turned, across, y_up, y_up_across, y_down, y_down_across]
    row_parts += [*y_opposite, *y_opposite_across]
    col_shards = [
        (genotypes, beside, own_twin, twin(beside)),
        (z_up, z_up_side, z_up_twin, twin(z_up_side)),
        (z_down, z_down_side, z_down_twin, twin(z_down_side)),
        (z_opposite, z_opposite_side, twin(z_opposite), twin(z_opposite_side)),
    ]

    away = (jnp.arange(4, dtype=jnp.uint32) - z) & 3
    slots = jnp.where(away == 0, 0, jnp.where(away == 1, 2, jnp.where(away == 2, 3, 1)))
    slots = slots.astype(jnp.int32)
    pick = slots[0] * 4 + (core * 2 + x_lo).astype(jnp.int32)
    pick = jnp.stack([pick, *[jnp.int32(step) for step in STEP_OF_SLOT]])
    flat_shards = [shard for group in col_shards for shard in group]
    factor = panel(pick, running[:, 0, 0, :], inverse, row_parts, flat_shards)
    pieces = factor.reshape(NY, NH, 128, NB)
    heard = lax.ppermute(pieces[:, 1], "col", [(0, 1)])
    pieces = jnp.where(x_hi == 0, pieces[:, 0], heard)
    heard = sum(
        lax.ppermute(pieces[d], "col", [(h, d * NH + h) for h in range(NH)]) for d in range(1, NY)
    )
    own_factor = jnp.where(y == 0, pieces[0], heard)
    pair = jnp.stack([own_factor, lax.ppermute(own_factor, "col", col_perm(0, 1))])
    row_factor = jnp.concatenate(ring_direct(pair, "col", col_perm), axis=0).reshape(1024, NB)
    pair = jnp.stack([own_factor, lax.ppermute(own_factor, "row", row_perm(0, 1, 0))])
    half = jnp.stack(ring_direct(pair, "row", row_perm))
    half_twin = lax.ppermute(half, "row", row_perm(0, 0, 1))
    high, low = split_bf16(jnp.stack([half, half_twin], axis=1).reshape(2048, NB).T)
    col_factor = jnp.concatenate([high, low, high], axis=0)

    tiles = jnp.arange(16, dtype=jnp.uint32)
    hit = grid_map[None, :] == jnp.arange(16, dtype=jnp.int32)[:, None]
    inverse_map = jnp.sum(jnp.where(hit, tiles[None, :], 0), axis=1).astype(jnp.uint32)
    step_y = ((inverse_map >> 2) - y) & 3
    slot = jnp.where(step_y == 0, 0, jnp.where(step_y == 1, 2, jnp.where(step_y == 2, 3, 1)))
    tile = ((slot.astype(jnp.uint32) * 2) + (((inverse_map >> 1) & 1) ^ x_hi)) * 2 + (inverse_map & 1)
    row_start = row_index * 1024 + inverse_map * 64
    side = jnp.arange(4, dtype=jnp.uint32)
    place = (((side & 1) ^ x_lo) << 1) + ((side >> 1) ^ core)
    is_col0 = jnp.where(col_index == 0, 1, 0).astype(jnp.uint32)
    table = jnp.concatenate(
        [inverse_map, tile, row_start, place, slots.astype(jnp.uint32), is_col0[None]]
    ).astype(jnp.int32)

    result, packed = None, factor
    running = running.reshape(1024, 16, 128)
    for part in range(2):
        late_rows, packed = lax.optimization_barrier((row_parts, packed))
        prods = []
        for plane in (2 * part, 2 * part + 1):
            prods.append(product(plane, slots, late_rows, flat_shards))
        packed = epilogue(part, table, running, prods, row_factor, col_factor, snp_count)
        coded = lax.all_to_all(
            packed.reshape(16, CODED_ROWS, 128), "row", split_axis=0, concat_axis=0, tiled=True
        )
        result = unpack(part, coded, result)
    return result.reshape(16, 1, 64, 16, 1, 128)


def solution(mesh):
    in_specs = (P(None, ("row", "col")), P("row", None, "col", None), P())
    out_specs = P(None, "row", None, None, "col", None)
    return jax.shard_map(
        compute, mesh=mesh, in_specs=in_specs, out_specs=out_specs, check_vma=False
    )
```

```python
import jax
import jax.numpy as jnp
from jax import lax
from jax.experimental import pallas as pl
from jax.experimental.pallas import tpu as pltpu
from jax.sharding import PartitionSpec as P


NB = 128
NZ, NX, NC = 4, 2, 2
NY, NH = 4, 2
STEP_OF_SLOT = (0, 3, 1, 2)
TILE_ROWS = 64
HALF = 8
PAIRS = TILE_ROWS * HALF // 16
TILES_STEP = 2
CODED_ROWS = TILE_ROWS * HALF + 16
LEVELS = 32767.0
LOG_STEP = 0.6931471805599453 / 64.0


def row_perm(dz=0, fx=0, fc=0):
    return [
        ((z * NX + x) * NC + k, (((z + dz) % NZ) * NX + (x ^ fx)) * NC + (k ^ fc))
        for z in range(NZ)
        for x in range(NX)
        for k in range(NC)
    ]


def col_perm(dy=0, fh=0):
    return [(y * NH + h, ((y + dy) % NY) * NH + (h ^ fh)) for y in range(NY) for h in range(NH)]


def ring_sides(shard, axis, perm):
    return lax.ppermute(shard, axis, perm(1)), lax.ppermute(shard, axis, perm(-1))


def ring_relay(up, down, axis, perm):
    half = up.shape[0] // 2
    top = lax.ppermute(up[:half], axis, perm(1))
    bottom = lax.ppermute(down[half:], axis, perm(-1))
    return top, bottom


def ring_direct(shard, axis, perm):
    return [shard] + [lax.ppermute(shard, axis, perm(d)) for d in (1, -1, 2)]


def split_bf16(value):
    high = lax.reduce_precision(value, exponent_bits=8, mantissa_bits=7)
    return high.astype(jnp.bfloat16), (value - high).astype(jnp.bfloat16)


def epilogue_kernel(table, *refs, part, inv_snp):
    tiles, (col_factor0, col_factor1, out, values) = refs[: 4 * TILES_STEP], refs[4 * TILES_STEP :]
    for n in range(TILES_STEP):
        running, prod0, prod1, row_factor = tiles[n * 4 : (n + 1) * 4]
        row_start = table[32 + pl.program_id(0) * TILES_STEP + n]
        old_rows = running.reshape(TILE_ROWS * HALF, 128)
        mine = row_factor[...]
        high = mine.astype(jnp.bfloat16)
        low = (mine - high.astype(jnp.float32)).astype(jnp.bfloat16)
        left = jnp.concatenate([high, high, low], axis=1)
        for plane, (prod, col_factor) in enumerate(((prod0, col_factor0), (prod1, col_factor1))):
            outer = jnp.dot(left, col_factor[...], preferred_element_type=jnp.float32)
            for side in range(4):
                place = table[48 + side] + plane * 4
                lanes = slice(side * 128, (side + 1) * 128)
                old = old_rows[pl.ds(place, TILE_ROWS, stride=HALF), :]
                values[n, pl.ds(place, TILE_ROWS, stride=HALF), :] = (
                    old + prod[:, lanes] * inv_snp - outer[:, lanes]
                )

        @pl.when(row_start < NB)
        def _():
            values[n] = jnp.zeros((TILE_ROWS * HALF, 128), jnp.float32)

        if part == 0:

            @pl.when(table[56] == 1)
            def _():
                row_pos = row_start + lax.broadcasted_iota(jnp.int32, (TILE_ROWS, NB), 0)
                lane = lax.broadcasted_iota(jnp.int32, (TILE_ROWS, NB), 1)
                values[n, pl.ds(0, TILE_ROWS, stride=HALF), :] = jnp.where(
                    row_pos >= lane, mine, 0.0
                )

    for n in range(TILES_STEP):
        peak = jnp.full((16, 128), 1e-30, jnp.float32)
        for a in range(PAIRS):
            peak = jnp.maximum(peak, jnp.abs(values[n, a * 16 : (a + 1) * 16, :]))
        peak = jnp.maximum(peak[:8], peak[8:])
        code = jnp.minimum(jnp.ceil(jnp.log(peak) * (1.0 / LOG_STEP)) + 1.0, 8190.0)
        code = jnp.concatenate([code, code], axis=0)
        gain = LEVELS / jnp.exp(code * LOG_STEP)
        base = n * CODED_ROWS
        for a in range(PAIRS):
            scaled = jnp.round(values[n, a * 16 : (a + 1) * 16, :] * gain)
            out[base + a * 16 : base + (a + 1) * 16, :] = scaled.astype(jnp.int32).astype(jnp.int16)
        last = base + TILE_ROWS * HALF
        out[last : last + 16, :] = code.astype(jnp.int32).astype(jnp.int16)


def epilogue(part, table, running, prods, row_factor, col_factor, snp_count):
    specs, arrays = [], []
    for n in range(TILES_STEP):
        block = pl.BlockSpec((TILE_ROWS, 512), lambda i, t, n=n: (t[16 + i * TILES_STEP + n], 0))
        specs += [
            pl.BlockSpec(
                (TILE_ROWS, HALF, 128), lambda i, t, n=n: (t[i * TILES_STEP + n], part, 0)
            ),
            block,
            block,
            pl.BlockSpec((TILE_ROWS, NB), lambda i, t, n=n: (t[16 + i * TILES_STEP + n], 0)),
        ]
        arrays += [running, *prods, row_factor]
    return pl.pallas_call(
        lambda *refs: epilogue_kernel(*refs, part=part, inv_snp=1.0 / snp_count),
        grid_spec=pltpu.PrefetchScalarGridSpec(
            num_scalar_prefetch=1,
            grid=(16 // TILES_STEP,),
            in_specs=[
                *specs,
                pl.BlockSpec((3 * NB, 512), lambda i, t: (0, t[52 + part * 2])),
                pl.BlockSpec((3 * NB, 512), lambda i, t: (0, t[53 + part * 2])),
            ],
            out_specs=pl.BlockSpec((TILES_STEP * CODED_ROWS, 128), lambda i, t: (i, 0)),
            scratch_shapes=[pltpu.VMEM((TILES_STEP, TILE_ROWS * HALF, 128), jnp.float32)],
        ),
        out_shape=jax.ShapeDtypeStruct((16 * CODED_ROWS, 128), jnp.int16),
        name="epilogue",
    )(table, *arrays, col_factor, col_factor)


ROW_STEP = 256
ROW_PLACES = ((0, 0, 0), (0, 1, 128), (1, 2, 0), (1, 3, 128), (2, 4, 0), (2, 5, 128))
ROW_PLACES += ((3, 6, 0), (3, 7, 64), (3, 8, 128), (3, 9, 192))


def fetch_rows(parts, rows, sems):
    step = pl.program_id(0)

    def copies(n):
        places = [(part, row) for where, part, row in ROW_PLACES if where == n]
        return [
            pltpu.make_async_copy(
                parts[part],
                rows.at[n % 2, row : row + parts[part].shape[0], :],
                sems.at[n % 2, number],
            )
            for number, (part, row) in enumerate(places)
        ]

    for n in range(4):

        @pl.when(step == n)
        def _():
            if n == 0:
                for copy in copies(0):
                    copy.start()
            if n < 3:
                for copy in copies(n + 1):
                    copy.start()
            for copy in copies(n):
                copy.wait()


def product_kernel(slots, *refs, plane):
    parts, shards, (out, rows, cols, row_sems, col_sems) = refs[:10], refs[10:26], refs[26:]
    first = pl.program_id(0) == 0

    def copy(slot, side):
        return pltpu.make_async_copy(
            shards[slot * 4 + side], cols.at[:, side * 128 : (side + 1) * 128], col_sems.at[side]
        )

    for slot in range(4):

        @pl.when(jnp.logical_and(first, slots[plane] == slot))
        def _():
            for side in range(4):
                copy(slot, side).start()

    fetch_rows(parts, rows, row_sems)

    @pl.when(first)
    def _():
        for side in range(4):
            copy(0, side).wait()

    out[...] = jnp.dot(
        rows[pl.program_id(0) % 2], cols[...], preferred_element_type=jnp.float32
    )


def product(plane, slots, parts, shards):
    count = shards[0].shape[0]
    return pl.pallas_call(
        lambda *refs: product_kernel(*refs, plane=plane),
        grid_spec=pltpu.PrefetchScalarGridSpec(
            num_scalar_prefetch=1,
            grid=(4,),
            in_specs=[pl.BlockSpec(memory_space=pl.ANY)] * 26,
            out_specs=pl.BlockSpec((ROW_STEP, 512), lambda i, t: (i, 0)),
            scratch_shapes=[
                pltpu.VMEM((2, ROW_STEP, count), jnp.bfloat16),
                pltpu.VMEM((count, 512), jnp.bfloat16),
                pltpu.SemaphoreType.DMA((2, 4)),
                pltpu.SemaphoreType.DMA((4,)),
            ],
        ),
        out_shape=jax.ShapeDtypeStruct((4 * ROW_STEP, 512), jnp.float32),
        name="product",
    )(slots, *parts, *shards)


def panel_kernel(pick, old, inverse, *refs, inv_snp):
    parts, shards, (out, rows, first, row_sems, sem) = refs[:10], refs[10:26], refs[26:]

    @pl.when(pl.program_id(0) == 0)
    def _():
        for n in range(16):

            @pl.when(pick[0] == n)
            def _():
                copy = pltpu.make_async_copy(shards[n], first, sem)
                copy.start()
                copy.wait()

    fetch_rows(parts, rows, row_sems)
    product_rows = jnp.dot(
        rows[pl.program_id(0) % 2], first[...], preferred_element_type=jnp.float32
    )
    out[...] = lax.dot_general(
        old[...] + product_rows * inv_snp,
        inverse[...],
        (((1,), (1,)), ((), ())),
        precision=lax.Precision.HIGHEST,
        preferred_element_type=jnp.float32,
    )


def panel(pick, old, inverse, parts, shards):
    count = shards[0].shape[0]
    block = pl.BlockSpec((ROW_STEP, NB), lambda i, t: (t[1 + i], 0))
    return pl.pallas_call(
        lambda *refs: panel_kernel(*refs, inv_snp=1.0 / count),
        grid_spec=pltpu.PrefetchScalarGridSpec(
            num_scalar_prefetch=1,
            grid=(4,),
            in_specs=[
                block,
                pl.BlockSpec((NB, NB), lambda i, t: (0, 0)),
                *[pl.BlockSpec(memory_space=pl.ANY)] * 26,
            ],
            out_specs=block,
            scratch_shapes=[
                pltpu.VMEM((2, ROW_STEP, count), jnp.bfloat16),
                pltpu.VMEM((count, NB), jnp.bfloat16),
                pltpu.SemaphoreType.DMA((2, 4)),
                pltpu.SemaphoreType.DMA(()),
            ],
        ),
        out_shape=jax.ShapeDtypeStruct((4 * ROW_STEP, NB), jnp.float32),
        name="panel",
    )(pick, old, inverse, *parts, *shards)


def unpack_kernel(coded, *refs):
    out = refs[-1]
    for source in range(4):
        code = coded[source, TILE_ROWS * HALF :, :].astype(jnp.float32)
        scale = jnp.exp(code * LOG_STEP) * (1.0 / LEVELS)
        for a in range(PAIRS):
            values = coded[source, a * 16 : (a + 1) * 16, :].astype(jnp.float32) * scale
            row = source * TILE_ROWS + a * 2
            out[row : row + 2] = values.reshape(2, HALF, 128)


def unpack(part, coded, before):
    begun = [] if before is None else [before]
    return pl.pallas_call(
        unpack_kernel,
        grid=(4,),
        in_specs=[
            pl.BlockSpec((4, CODED_ROWS, 128), lambda i: (i, 0, 0)),
            *[pl.BlockSpec(memory_space=pl.ANY)] * len(begun),
        ],
        out_specs=pl.BlockSpec((4 * TILE_ROWS, HALF, 128), lambda i: (i, part, 0)),
        out_shape=jax.ShapeDtypeStruct((16 * TILE_ROWS, 2 * HALF, 128), jnp.float32),
        input_output_aliases={1: 0} if begun else {},
        name="unpack",
    )(coded, *begun)


def compute(genotypes, running, grid_map):
    row_index = lax.axis_index("row").astype(jnp.uint32)
    col_index = lax.axis_index("col").astype(jnp.uint32)
    z, x_lo, core = row_index >> 2, (row_index >> 1) & 1, row_index & 1
    y, x_hi = col_index >> 1, col_index & 1
    snp_count = genotypes.shape[0]
    inv_snp = 1.0 / snp_count

    def dot0(a, b):
        return lax.dot_general(a, b, (((0,), (0,)), ((), ())), preferred_element_type=jnp.float32)

    def twin(value):
        return lax.ppermute(value, "row", row_perm(0, 0, 1))

    z_up, z_down = ring_sides(genotypes, "row", row_perm)
    turned = genotypes.T
    across = lax.ppermute(turned, "col", col_perm(0, 1))
    y_up, y_down = ring_sides(turned, "col", col_perm)
    own_twin = twin(genotypes)

    leading = running[:NB, 0, 0, :] + dot0(genotypes, genotypes) * inv_snp
    lower = jnp.linalg.cholesky(leading)

    late, across, lower = lax.optimization_barrier((genotypes, across, lower))
    beside = lax.ppermute(late, "row", row_perm(0, 1, 0))
    y_up_across, y_down_across = ring_sides(across, "col", col_perm)
    z_opposite = jnp.concatenate(ring_relay(z_up, z_down, "row", row_perm), axis=0)
    y_opposite = ring_relay(y_up, y_down, "col", col_perm)
    z_up_twin, z_down_twin = twin(z_up), twin(z_down)
    inverse = lax.linalg.triangular_solve(
        lower, jnp.eye(NB, dtype=jnp.float32), left_side=True, lower=True
    )

    heard = sum(lax.ppermute(inverse, "row", [(0, d * NX * NC)]) for d in range(1, NZ))
    inverse = jnp.where(z == 0, inverse, heard)
    z_up_side, z_down_side = ring_sides(beside, "row", row_perm)
    heard = lax.ppermute(inverse, "row", [(d * NX * NC, d * NX * NC + NC) for d in range(NZ)])
    inverse = jnp.where(x_lo == 0, inverse, heard)
    z_opposite_side = lax.ppermute(z_opposite, "row", row_perm(0, 1, 0))
    y_opposite_across = ring_relay(y_up_across, y_down_across, "col", col_perm)
    heard = lax.ppermute(inverse, "row", [(d * NC, d * NC + 1) for d in range(NZ * NX)])
    inverse = jnp.where(core == 0, inverse, heard)

    row_parts = [turned, across, y_up, y_up_across, y_down, y_down_across]
    row_parts += [*y_opposite, *y_opposite_across]
    col_shards = [
        (genotypes, beside, own_twin, twin(beside)),
        (z_up, z_up_side, z_up_twin, twin(z_up_side)),
        (z_down, z_down_side, z_down_twin, twin(z_down_side)),
        (z_opposite, z_opposite_side, twin(z_opposite), twin(z_opposite_side)),
    ]

    away = (jnp.arange(4, dtype=jnp.uint32) - z) & 3
    slots = jnp.where(away == 0, 0, jnp.where(away == 1, 2, jnp.where(away == 2, 3, 1)))
    slots = slots.astype(jnp.int32)
    pick = slots[0] * 4 + (core * 2 + x_lo).astype(jnp.int32)
    pick = jnp.stack([pick, *[jnp.int32(step) for step in STEP_OF_SLOT]])
    flat_shards = [shard for group in col_shards for shard in group]
    factor = panel(pick, running[:, 0, 0, :], inverse, row_parts, flat_shards)
    pieces = factor.reshape(NY, NH, 128, NB)
    heard = lax.ppermute(pieces[:, 1], "col", [(0, 1)])
    pieces = jnp.where(x_hi == 0, pieces[:, 0], heard)
    heard = sum(
        lax.ppermute(pieces[d], "col", [(h, d * NH + h) for h in range(NH)]) for d in range(1, NY)
    )
    own_factor = jnp.where(y == 0, pieces[0], heard)
    pair = jnp.stack([own_factor, lax.ppermute(own_factor, "col", col_perm(0, 1))])
    row_factor = jnp.concatenate(ring_direct(pair, "col", col_perm), axis=0).reshape(1024, NB)
    pair = jnp.stack([own_factor, lax.ppermute(own_factor, "row", row_perm(0, 1, 0))])
    half = jnp.stack(ring_direct(pair, "row", row_perm))
    half_twin = lax.ppermute(half, "row", row_perm(0, 0, 1))
    high, low = split_bf16(jnp.stack([half, half_twin], axis=1).reshape(2048, NB).T)
    col_factor = jnp.concatenate([high, low, high], axis=0)

    tiles = jnp.arange(16, dtype=jnp.uint32)
    hit = grid_map[None, :] == jnp.arange(16, dtype=jnp.int32)[:, None]
    inverse_map = jnp.sum(jnp.where(hit, tiles[None, :], 0), axis=1).astype(jnp.uint32)
    step_y = ((inverse_map >> 2) - y) & 3
    slot = jnp.where(step_y == 0, 0, jnp.where(step_y == 1, 2, jnp.where(step_y == 2, 3, 1)))
    tile = ((slot.astype(jnp.uint32) * 2) + (((inverse_map >> 1) & 1) ^ x_hi)) * 2 + (inverse_map & 1)
    row_start = row_index * 1024 + inverse_map * 64
    side = jnp.arange(4, dtype=jnp.uint32)
    place = (((side & 1) ^ x_lo) << 1) + ((side >> 1) ^ core)
    is_col0 = jnp.where(col_index == 0, 1, 0).astype(jnp.uint32)
    table = jnp.concatenate(
        [inverse_map, tile, row_start, place, slots.astype(jnp.uint32), is_col0[None]]
    ).astype(jnp.int32)

    prods = []
    running = running.reshape(1024, 16, 128)
    late_rows, factor = lax.optimization_barrier((row_parts, factor))
    for plane in range(3):
        prods.append(product(plane, slots, late_rows, flat_shards))
    result = None
    for part in range(2):
        if part == 1:
            late_rows, packed = lax.optimization_barrier((row_parts, packed))
            prods.append(product(3, slots, late_rows, flat_shards))
        packed = epilogue(
            part, table, running, prods[2 * part : 2 * part + 2], row_factor, col_factor, snp_count
        )
        coded = lax.all_to_all(
            packed.reshape(16, CODED_ROWS, 128), "row", split_axis=0, concat_axis=0, tiled=True
        )
        result = unpack(part, coded, result)
    return result.reshape(16, 1, 64, 16, 1, 128)


def solution(mesh):
    in_specs = (P(None, ("row", "col")), P("row", None, "col", None), P())
    out_specs = P(None, "row", None, None, "col", None)
    return jax.shard_map(
        compute, mesh=mesh, in_specs=in_specs, out_specs=out_specs, check_vma=False
    )
```

```python
import jax
import jax.numpy as jnp
from jax import lax
from jax.experimental import pallas as pl
from jax.experimental.pallas import tpu as pltpu
from jax.sharding import PartitionSpec as P


NB = 128
NZ, NX, NC = 4, 2, 2
NY, NH = 4, 2
STEP_OF_SLOT = (0, 3, 1, 2)
TILE_ROWS = 64
HALF = 8
PAIRS = TILE_ROWS * HALF // 16
TILES_STEP = 2
CODED_ROWS = TILE_ROWS * HALF + 16
LEVELS = 32767.0
LOG_STEP = 0.6931471805599453 / 64.0


def row_perm(dz=0, fx=0, fc=0):
    return [
        ((z * NX + x) * NC + k, (((z + dz) % NZ) * NX + (x ^ fx)) * NC + (k ^ fc))
        for z in range(NZ)
        for x in range(NX)
        for k in range(NC)
    ]


def col_perm(dy=0, fh=0):
    return [(y * NH + h, ((y + dy) % NY) * NH + (h ^ fh)) for y in range(NY) for h in range(NH)]


def ring_sides(shard, axis, perm):
    return lax.ppermute(shard, axis, perm(1)), lax.ppermute(shard, axis, perm(-1))


def ring_relay(up, down, axis, perm):
    half = up.shape[0] // 2
    top = lax.ppermute(up[:half], axis, perm(1))
    bottom = lax.ppermute(down[half:], axis, perm(-1))
    return top, bottom


def ring_direct(shard, axis, perm):
    return [shard] + [lax.ppermute(shard, axis, perm(d)) for d in (1, -1, 2)]


def split_bf16(value):
    high = lax.reduce_precision(value, exponent_bits=8, mantissa_bits=7)
    return high.astype(jnp.bfloat16), (value - high).astype(jnp.bfloat16)


def epilogue_kernel(table, *refs, part, inv_snp):
    tiles, (col_factor0, col_factor1, out, values) = refs[: 4 * TILES_STEP], refs[4 * TILES_STEP :]
    for n in range(TILES_STEP):
        running, prod0, prod1, row_factor = tiles[n * 4 : (n + 1) * 4]
        row_start = table[32 + pl.program_id(0) * TILES_STEP + n]
        old_rows = running.reshape(TILE_ROWS * HALF, 128)
        mine = row_factor[...]
        high = mine.astype(jnp.bfloat16)
        low = (mine - high.astype(jnp.float32)).astype(jnp.bfloat16)
        left = jnp.concatenate([high, high, low], axis=1)
        for plane, (prod, col_factor) in enumerate(((prod0, col_factor0), (prod1, col_factor1))):
            outer = jnp.dot(left, col_factor[...], preferred_element_type=jnp.float32)
            for side in range(4):
                place = table[48 + side] + plane * 4
                lanes = slice(side * 128, (side + 1) * 128)
                old = old_rows[pl.ds(place, TILE_ROWS, stride=HALF), :]
                values[n, pl.ds(place, TILE_ROWS, stride=HALF), :] = (
                    old + prod[:, lanes] * inv_snp - outer[:, lanes]
                )

        @pl.when(row_start < NB)
        def _():
            values[n] = jnp.zeros((TILE_ROWS * HALF, 128), jnp.float32)

        if part == 0:

            @pl.when(table[56] == 1)
            def _():
                row_pos = row_start + lax.broadcasted_iota(jnp.int32, (TILE_ROWS, NB), 0)
                lane = lax.broadcasted_iota(jnp.int32, (TILE_ROWS, NB), 1)
                values[n, pl.ds(0, TILE_ROWS, stride=HALF), :] = jnp.where(
                    row_pos >= lane, mine, 0.0
                )

    for n in range(TILES_STEP):
        peak = jnp.full((16, 128), 1e-30, jnp.float32)
        for a in range(PAIRS):
            peak = jnp.maximum(peak, jnp.abs(values[n, a * 16 : (a + 1) * 16, :]))
        peak = jnp.maximum(peak[:8], peak[8:])
        code = jnp.minimum(jnp.ceil(jnp.log(peak) * (1.0 / LOG_STEP)) + 1.0, 8190.0)
        code = jnp.concatenate([code, code], axis=0)
        gain = LEVELS / jnp.exp(code * LOG_STEP)
        base = n * CODED_ROWS
        for a in range(PAIRS):
            scaled = jnp.round(values[n, a * 16 : (a + 1) * 16, :] * gain)
            out[base + a * 16 : base + (a + 1) * 16, :] = scaled.astype(jnp.int32).astype(jnp.int16)
        last = base + TILE_ROWS * HALF
        out[last : last + 16, :] = code.astype(jnp.int32).astype(jnp.int16)


def epilogue(part, table, running, prods, row_factor, col_factor, snp_count):
    specs, arrays = [], []
    for n in range(TILES_STEP):
        block = pl.BlockSpec((TILE_ROWS, 512), lambda i, t, n=n: (t[16 + i * TILES_STEP + n], 0))
        specs += [
            pl.BlockSpec(
                (TILE_ROWS, HALF, 128), lambda i, t, n=n: (t[i * TILES_STEP + n], part, 0)
            ),
            block,
            block,
            pl.BlockSpec((TILE_ROWS, NB), lambda i, t, n=n: (t[16 + i * TILES_STEP + n], 0)),
        ]
        arrays += [running, *prods, row_factor]
    return pl.pallas_call(
        lambda *refs: epilogue_kernel(*refs, part=part, inv_snp=1.0 / snp_count),
        grid_spec=pltpu.PrefetchScalarGridSpec(
            num_scalar_prefetch=1,
            grid=(16 // TILES_STEP,),
            in_specs=[
                *specs,
                pl.BlockSpec((3 * NB, 512), lambda i, t: (0, t[52 + part * 2])),
                pl.BlockSpec((3 * NB, 512), lambda i, t: (0, t[53 + part * 2])),
            ],
            out_specs=pl.BlockSpec((TILES_STEP * CODED_ROWS, 128), lambda i, t: (i, 0)),
            scratch_shapes=[pltpu.VMEM((TILES_STEP, TILE_ROWS * HALF, 128), jnp.float32)],
        ),
        out_shape=jax.ShapeDtypeStruct((16 * CODED_ROWS, 128), jnp.int16),
        name="epilogue",
    )(table, *arrays, col_factor, col_factor)


ROW_STEP = 256
ROW_PLACES = ((0, 0, 0), (0, 1, 128), (1, 2, 0), (1, 3, 128), (2, 4, 0), (2, 5, 128))
ROW_PLACES += ((3, 6, 0), (3, 7, 64), (3, 8, 128), (3, 9, 192))


def fetch_rows(parts, rows, sems):
    step = pl.program_id(0)

    def copies(n):
        places = [(part, row) for where, part, row in ROW_PLACES if where == n]
        return [
            pltpu.make_async_copy(
                parts[part],
                rows.at[n % 2, row : row + parts[part].shape[0], :],
                sems.at[n % 2, number],
            )
            for number, (part, row) in enumerate(places)
        ]

    for n in range(4):

        @pl.when(step == n)
        def _():
            if n == 0:
                for copy in copies(0):
                    copy.start()
            if n < 3:
                for copy in copies(n + 1):
                    copy.start()
            for copy in copies(n):
                copy.wait()


def product_kernel(slots, *refs, plane):
    parts, shards, (out, rows, cols, row_sems, col_sems) = refs[:10], refs[10:26], refs[26:]
    first = pl.program_id(0) == 0

    def copy(slot, side):
        return pltpu.make_async_copy(
            shards[slot * 4 + side], cols.at[:, side * 128 : (side + 1) * 128], col_sems.at[side]
        )

    for slot in range(4):

        @pl.when(jnp.logical_and(first, slots[plane] == slot))
        def _():
            for side in range(4):
                copy(slot, side).start()

    fetch_rows(parts, rows, row_sems)

    @pl.when(first)
    def _():
        for side in range(4):
            copy(0, side).wait()

    out[...] = jnp.dot(
        rows[pl.program_id(0) % 2], cols[...], preferred_element_type=jnp.float32
    )


def product(plane, slots, parts, shards):
    count = shards[0].shape[0]
    return pl.pallas_call(
        lambda *refs: product_kernel(*refs, plane=plane),
        grid_spec=pltpu.PrefetchScalarGridSpec(
            num_scalar_prefetch=1,
            grid=(4,),
            in_specs=[pl.BlockSpec(memory_space=pl.ANY)] * 26,
            out_specs=pl.BlockSpec((ROW_STEP, 512), lambda i, t: (i, 0)),
            scratch_shapes=[
                pltpu.VMEM((2, ROW_STEP, count), jnp.bfloat16),
                pltpu.VMEM((count, 512), jnp.bfloat16),
                pltpu.SemaphoreType.DMA((2, 4)),
                pltpu.SemaphoreType.DMA((4,)),
            ],
        ),
        out_shape=jax.ShapeDtypeStruct((4 * ROW_STEP, 512), jnp.float32),
        name="product",
    )(slots, *parts, *shards)


def panel_kernel(pick, old, inverse, *refs, inv_snp):
    parts, shards, (out, rows, first, row_sems, sem) = refs[:10], refs[10:26], refs[26:]

    @pl.when(pl.program_id(0) == 0)
    def _():
        for n in range(16):

            @pl.when(pick[0] == n)
            def _():
                pltpu.make_async_copy(shards[n], first, sem).start()

    fetch_rows(parts, rows, row_sems)

    @pl.when(pl.program_id(0) == 0)
    def _():
        pltpu.make_async_copy(shards[0], first, sem).wait()

    product_rows = jnp.dot(
        rows[pl.program_id(0) % 2], first[...], preferred_element_type=jnp.float32
    )
    out[...] = lax.dot_general(
        old[...] + product_rows * inv_snp,
        inverse[...],
        (((1,), (1,)), ((), ())),
        precision=lax.Precision.HIGHEST,
        preferred_element_type=jnp.float32,
    )


def panel(pick, old, inverse, parts, shards):
    count = shards[0].shape[0]
    block = pl.BlockSpec((ROW_STEP, NB), lambda i, t: (t[1 + i], 0))
    return pl.pallas_call(
        lambda *refs: panel_kernel(*refs, inv_snp=1.0 / count),
        grid_spec=pltpu.PrefetchScalarGridSpec(
            num_scalar_prefetch=1,
            grid=(4,),
            in_specs=[
                block,
                pl.BlockSpec((NB, NB), lambda i, t: (0, 0)),
                *[pl.BlockSpec(memory_space=pl.ANY)] * 26,
            ],
            out_specs=block,
            scratch_shapes=[
                pltpu.VMEM((2, ROW_STEP, count), jnp.bfloat16),
                pltpu.VMEM((count, NB), jnp.bfloat16),
                pltpu.SemaphoreType.DMA((2, 4)),
                pltpu.SemaphoreType.DMA(()),
            ],
        ),
        out_shape=jax.ShapeDtypeStruct((4 * ROW_STEP, NB), jnp.float32),
        name="panel",
    )(pick, old, inverse, *parts, *shards)


def unpack_kernel(coded, *refs):
    out = refs[-1]
    for source in range(4):
        code = coded[source, TILE_ROWS * HALF :, :].astype(jnp.float32)
        scale = jnp.exp(code * LOG_STEP) * (1.0 / LEVELS)
        for a in range(PAIRS):
            values = coded[source, a * 16 : (a + 1) * 16, :].astype(jnp.float32) * scale
            row = source * TILE_ROWS + a * 2
            out[row : row + 2] = values.reshape(2, HALF, 128)


def unpack(part, coded, before):
    begun = [] if before is None else [before]
    return pl.pallas_call(
        unpack_kernel,
        grid=(4,),
        in_specs=[
            pl.BlockSpec((4, CODED_ROWS, 128), lambda i: (i, 0, 0)),
            *[pl.BlockSpec(memory_space=pl.ANY)] * len(begun),
        ],
        out_specs=pl.BlockSpec((4 * TILE_ROWS, HALF, 128), lambda i: (i, part, 0)),
        out_shape=jax.ShapeDtypeStruct((16 * TILE_ROWS, 2 * HALF, 128), jnp.float32),
        input_output_aliases={1: 0} if begun else {},
        name="unpack",
    )(coded, *begun)


def compute(genotypes, running, grid_map):
    row_index = lax.axis_index("row").astype(jnp.uint32)
    col_index = lax.axis_index("col").astype(jnp.uint32)
    z, x_lo, core = row_index >> 2, (row_index >> 1) & 1, row_index & 1
    y, x_hi = col_index >> 1, col_index & 1
    snp_count = genotypes.shape[0]
    inv_snp = 1.0 / snp_count

    def dot0(a, b):
        return lax.dot_general(a, b, (((0,), (0,)), ((), ())), preferred_element_type=jnp.float32)

    def twin(value):
        return lax.ppermute(value, "row", row_perm(0, 0, 1))

    z_up, z_down = ring_sides(genotypes, "row", row_perm)
    turned = genotypes.T
    across = lax.ppermute(turned, "col", col_perm(0, 1))
    y_up, y_down = ring_sides(turned, "col", col_perm)
    own_twin = twin(genotypes)

    leading = running[:NB, 0, 0, :] + dot0(genotypes, genotypes) * inv_snp
    lower = jnp.linalg.cholesky(leading)
    inverse = lax.linalg.triangular_solve(
        lower, jnp.eye(NB, dtype=jnp.float32), left_side=True, lower=True
    )

    away = (jnp.arange(4, dtype=jnp.uint32) - z) & 3
    slots = jnp.where(away == 0, 0, jnp.where(away == 1, 2, jnp.where(away == 2, 3, 1)))
    slots = slots.astype(jnp.int32)
    pick = slots[0] * 4 + (core * 2 + x_lo).astype(jnp.int32)
    pick = jnp.stack([pick, *[jnp.int32(step) for step in STEP_OF_SLOT]])

    late, across, inverse, old_panel, pick, slots = lax.optimization_barrier(
        (genotypes, across, inverse, running[:, 0, 0, :], pick, slots)
    )
    beside = lax.ppermute(late, "row", row_perm(0, 1, 0))
    y_up_across, y_down_across = ring_sides(across, "col", col_perm)
    z_opposite = jnp.concatenate(ring_relay(z_up, z_down, "row", row_perm), axis=0)
    y_opposite = ring_relay(y_up, y_down, "col", col_perm)
    z_up_twin, z_down_twin = twin(z_up), twin(z_down)

    heard = sum(lax.ppermute(inverse, "row", [(0, d * NX * NC)]) for d in range(1, NZ))
    inverse = jnp.where(z == 0, inverse, heard)
    z_up_side, z_down_side = ring_sides(beside, "row", row_perm)
    heard = lax.ppermute(inverse, "row", [(d * NX * NC, d * NX * NC + NC) for d in range(NZ)])
    inverse = jnp.where(x_lo == 0, inverse, heard)
    z_opposite_side = lax.ppermute(z_opposite, "row", row_perm(0, 1, 0))
    y_opposite_across = ring_relay(y_up_across, y_down_across, "col", col_perm)
    heard = lax.ppermute(inverse, "row", [(d * NC, d * NC + 1) for d in range(NZ * NX)])
    inverse = jnp.where(core == 0, inverse, heard)

    row_parts = [turned, across, y_up, y_up_across, y_down, y_down_across]
    row_parts += [*y_opposite, *y_opposite_across]
    col_shards = [
        (genotypes, beside, own_twin, twin(beside)),
        (z_up, z_up_side, z_up_twin, twin(z_up_side)),
        (z_down, z_down_side, z_down_twin, twin(z_down_side)),
        (z_opposite, z_opposite_side, twin(z_opposite), twin(z_opposite_side)),
    ]

    flat_shards = [shard for group in col_shards for shard in group]
    factor = panel(pick, old_panel, inverse, row_parts, flat_shards)
    pieces = factor.reshape(NY, NH, 128, NB)
    heard = lax.ppermute(pieces[:, 1], "col", [(0, 1)])
    pieces = jnp.where(x_hi == 0, pieces[:, 0], heard)
    heard = sum(
        lax.ppermute(pieces[d], "col", [(h, d * NH + h) for h in range(NH)]) for d in range(1, NY)
    )
    own_factor = jnp.where(y == 0, pieces[0], heard)
    pair = jnp.stack([own_factor, lax.ppermute(own_factor, "col", col_perm(0, 1))])
    row_factor = jnp.concatenate(ring_direct(pair, "col", col_perm), axis=0).reshape(1024, NB)
    pair = jnp.stack([own_factor, lax.ppermute(own_factor, "row", row_perm(0, 1, 0))])
    half = jnp.stack(ring_direct(pair, "row", row_perm))
    half_twin = lax.ppermute(half, "row", row_perm(0, 0, 1))
    high, low = split_bf16(jnp.stack([half, half_twin], axis=1).reshape(2048, NB).T)
    col_factor = jnp.concatenate([high, low, high], axis=0)

    tiles = jnp.arange(16, dtype=jnp.uint32)
    hit = grid_map[None, :] == jnp.arange(16, dtype=jnp.int32)[:, None]
    inverse_map = jnp.sum(jnp.where(hit, tiles[None, :], 0), axis=1).astype(jnp.uint32)
    step_y = ((inverse_map >> 2) - y) & 3
    slot = jnp.where(step_y == 0, 0, jnp.where(step_y == 1, 2, jnp.where(step_y == 2, 3, 1)))
    tile = ((slot.astype(jnp.uint32) * 2) + (((inverse_map >> 1) & 1) ^ x_hi)) * 2 + (inverse_map & 1)
    row_start = row_index * 1024 + inverse_map * 64
    side = jnp.arange(4, dtype=jnp.uint32)
    place = (((side & 1) ^ x_lo) << 1) + ((side >> 1) ^ core)
    is_col0 = jnp.where(col_index == 0, 1, 0).astype(jnp.uint32)
    table = jnp.concatenate(
        [inverse_map, tile, row_start, place, slots.astype(jnp.uint32), is_col0[None]]
    ).astype(jnp.int32)

    prods = []
    running = running.reshape(1024, 16, 128)
    late_rows, factor = lax.optimization_barrier((row_parts, factor))
    for plane in range(3):
        prods.append(product(plane, slots, late_rows, flat_shards))
    result = None
    for part in range(2):
        if part == 1:
            late_rows, packed = lax.optimization_barrier((row_parts, packed))
            prods.append(product(3, slots, late_rows, flat_shards))
        packed = epilogue(
            part, table, running, prods[2 * part : 2 * part + 2], row_factor, col_factor, snp_count
        )
        coded = lax.all_to_all(
            packed.reshape(16, CODED_ROWS, 128), "row", split_axis=0, concat_axis=0, tiled=True
        )
        result = unpack(part, coded, result)
    return result.reshape(16, 1, 64, 16, 1, 128)


def solution(mesh):
    in_specs = (P(None, ("row", "col")), P("row", None, "col", None), P())
    out_specs = P(None, "row", None, None, "col", None)
    return jax.shard_map(
        compute, mesh=mesh, in_specs=in_specs, out_specs=out_specs, check_vma=False
    )
```

```python
import jax
import jax.numpy as jnp
from jax import lax
from jax.experimental import pallas as pl
from jax.experimental.pallas import tpu as pltpu
from jax.sharding import PartitionSpec as P


NB = 128
NZ, NX, NC = 4, 2, 2
NY, NH = 4, 2
STEP_OF_SLOT = (0, 3, 1, 2)
TILE_ROWS = 64
HALF = 8
PAIRS = TILE_ROWS * HALF // 16
TILES_STEP = 2
CODED_ROWS = TILE_ROWS * HALF + 16
LEVELS = 32767.0
LOG_STEP = 0.6931471805599453 / 64.0


def row_perm(dz=0, fx=0, fc=0):
    return [
        ((z * NX + x) * NC + k, (((z + dz) % NZ) * NX + (x ^ fx)) * NC + (k ^ fc))
        for z in range(NZ)
        for x in range(NX)
        for k in range(NC)
    ]


def col_perm(dy=0, fh=0):
    return [(y * NH + h, ((y + dy) % NY) * NH + (h ^ fh)) for y in range(NY) for h in range(NH)]


def ring_sides(shard, axis, perm):
    return lax.ppermute(shard, axis, perm(1)), lax.ppermute(shard, axis, perm(-1))


def ring_relay(up, down, axis, perm):
    half = up.shape[0] // 2
    top = lax.ppermute(up[:half], axis, perm(1))
    bottom = lax.ppermute(down[half:], axis, perm(-1))
    return top, bottom


def ring_direct(shard, axis, perm):
    return [shard] + [lax.ppermute(shard, axis, perm(d)) for d in (1, -1, 2)]


def split_bf16(value):
    high = lax.reduce_precision(value, exponent_bits=8, mantissa_bits=7)
    return high.astype(jnp.bfloat16), (value - high).astype(jnp.bfloat16)


def epilogue_kernel(table, *refs, part, inv_snp):
    tiles, (col_factor0, col_factor1, out, values) = refs[: 4 * TILES_STEP], refs[4 * TILES_STEP :]
    for n in range(TILES_STEP):
        running, prod0, prod1, row_factor = tiles[n * 4 : (n + 1) * 4]
        row_start = table[32 + pl.program_id(0) * TILES_STEP + n]
        old_rows = running.reshape(TILE_ROWS * HALF, 128)
        mine = row_factor[...]
        high = mine.astype(jnp.bfloat16)
        low = (mine - high.astype(jnp.float32)).astype(jnp.bfloat16)
        left = jnp.concatenate([high, high, low], axis=1)
        for plane, (prod, col_factor) in enumerate(((prod0, col_factor0), (prod1, col_factor1))):
            outer = jnp.dot(left, col_factor[...], preferred_element_type=jnp.float32)
            for side in range(4):
                place = table[48 + side] + plane * 4
                lanes = slice(side * 128, (side + 1) * 128)
                old = old_rows[pl.ds(place, TILE_ROWS, stride=HALF), :]
                values[n, pl.ds(place, TILE_ROWS, stride=HALF), :] = (
                    old + prod[:, lanes] * inv_snp - outer[:, lanes]
                )

        @pl.when(row_start < NB)
        def _():
            values[n] = jnp.zeros((TILE_ROWS * HALF, 128), jnp.float32)

        if part == 0:

            @pl.when(table[56] == 1)
            def _():
                row_pos = row_start + lax.broadcasted_iota(jnp.int32, (TILE_ROWS, NB), 0)
                lane = lax.broadcasted_iota(jnp.int32, (TILE_ROWS, NB), 1)
                values[n, pl.ds(0, TILE_ROWS, stride=HALF), :] = jnp.where(
                    row_pos >= lane, mine, 0.0
                )

    for n in range(TILES_STEP):
        peak = jnp.full((16, 128), 1e-30, jnp.float32)
        for a in range(PAIRS):
            peak = jnp.maximum(peak, jnp.abs(values[n, a * 16 : (a + 1) * 16, :]))
        peak = jnp.maximum(peak[:8], peak[8:])
        code = jnp.minimum(jnp.ceil(jnp.log(peak) * (1.0 / LOG_STEP)) + 1.0, 8190.0)
        code = jnp.concatenate([code, code], axis=0)
        gain = LEVELS / jnp.exp(code * LOG_STEP)
        base = n * CODED_ROWS
        for a in range(PAIRS):
            scaled = jnp.round(values[n, a * 16 : (a + 1) * 16, :] * gain)
            out[base + a * 16 : base + (a + 1) * 16, :] = scaled.astype(jnp.int32).astype(jnp.int16)
        last = base + TILE_ROWS * HALF
        out[last : last + 16, :] = code.astype(jnp.int32).astype(jnp.int16)


def epilogue(part, table, running, prods, row_factor, col_factor, snp_count):
    specs, arrays = [], []
    for n in range(TILES_STEP):
        block = pl.BlockSpec((TILE_ROWS, 512), lambda i, t, n=n: (t[16 + i * TILES_STEP + n], 0))
        specs += [
            pl.BlockSpec(
                (TILE_ROWS, HALF, 128), lambda i, t, n=n: (t[i * TILES_STEP + n], part, 0)
            ),
            block,
            block,
            pl.BlockSpec((TILE_ROWS, NB), lambda i, t, n=n: (t[16 + i * TILES_STEP + n], 0)),
        ]
        arrays += [running, *prods, row_factor]
    return pl.pallas_call(
        lambda *refs: epilogue_kernel(*refs, part=part, inv_snp=1.0 / snp_count),
        grid_spec=pltpu.PrefetchScalarGridSpec(
            num_scalar_prefetch=1,
            grid=(16 // TILES_STEP,),
            in_specs=[
                *specs,
                pl.BlockSpec((3 * NB, 512), lambda i, t: (0, t[52 + part * 2])),
                pl.BlockSpec((3 * NB, 512), lambda i, t: (0, t[53 + part * 2])),
            ],
            out_specs=pl.BlockSpec((TILES_STEP * CODED_ROWS, 128), lambda i, t: (i, 0)),
            scratch_shapes=[pltpu.VMEM((TILES_STEP, TILE_ROWS * HALF, 128), jnp.float32)],
        ),
        out_shape=jax.ShapeDtypeStruct((16 * CODED_ROWS, 128), jnp.int16),
        name="epilogue",
    )(table, *arrays, col_factor, col_factor)


ROW_STEP = 256
ROW_PLACES = ((0, 0, 0), (0, 1, 128), (1, 2, 0), (1, 3, 128), (2, 4, 0), (2, 5, 128))
ROW_PLACES += ((3, 6, 0), (3, 7, 64), (3, 8, 128), (3, 9, 192))


def fetch_rows(parts, rows, sems):
    step = pl.program_id(0)

    def copies(n):
        places = [(part, row) for where, part, row in ROW_PLACES if where == n]
        return [
            pltpu.make_async_copy(
                parts[part],
                rows.at[n % 2, row : row + parts[part].shape[0], :],
                sems.at[n % 2, number],
            )
            for number, (part, row) in enumerate(places)
        ]

    for n in range(4):

        @pl.when(step == n)
        def _():
            if n == 0:
                for copy in copies(0):
                    copy.start()
            if n < 3:
                for copy in copies(n + 1):
                    copy.start()
            for copy in copies(n):
                copy.wait()


def product_kernel(slots, *refs, plane):
    parts, shards, (out, rows, cols, row_sems, col_sems) = refs[:10], refs[10:26], refs[26:]
    first = pl.program_id(0) == 0

    def copy(slot, side):
        return pltpu.make_async_copy(
            shards[slot * 4 + side], cols.at[:, side * 128 : (side + 1) * 128], col_sems.at[side]
        )

    for slot in range(4):

        @pl.when(jnp.logical_and(first, slots[plane] == slot))
        def _():
            for side in range(4):
                copy(slot, side).start()

    fetch_rows(parts, rows, row_sems)

    @pl.when(first)
    def _():
        for side in range(4):
            copy(0, side).wait()

    out[...] = jnp.dot(
        rows[pl.program_id(0) % 2], cols[...], preferred_element_type=jnp.float32
    )


def product(plane, slots, parts, shards):
    count = shards[0].shape[0]
    return pl.pallas_call(
        lambda *refs: product_kernel(*refs, plane=plane),
        grid_spec=pltpu.PrefetchScalarGridSpec(
            num_scalar_prefetch=1,
            grid=(4,),
            in_specs=[pl.BlockSpec(memory_space=pl.ANY)] * 26,
            out_specs=pl.BlockSpec((ROW_STEP, 512), lambda i, t: (i, 0)),
            scratch_shapes=[
                pltpu.VMEM((2, ROW_STEP, count), jnp.bfloat16),
                pltpu.VMEM((count, 512), jnp.bfloat16),
                pltpu.SemaphoreType.DMA((2, 4)),
                pltpu.SemaphoreType.DMA((4,)),
            ],
        ),
        out_shape=jax.ShapeDtypeStruct((4 * ROW_STEP, 512), jnp.float32),
        name="product",
    )(slots, *parts, *shards)


def panel_kernel(pick, old, inverse, *refs, inv_snp):
    parts, shards, (out, rows, first, row_sems, sem) = refs[:10], refs[10:26], refs[26:]

    @pl.when(pl.program_id(0) == 0)
    def _():
        for n in range(16):

            @pl.when(pick[0] == n)
            def _():
                pltpu.make_async_copy(shards[n], first, sem).start()

    fetch_rows(parts, rows, row_sems)

    @pl.when(pl.program_id(0) == 0)
    def _():
        pltpu.make_async_copy(shards[0], first, sem).wait()

    product_rows = jnp.dot(
        rows[pl.program_id(0) % 2], first[...], preferred_element_type=jnp.float32
    )
    out[...] = lax.dot_general(
        old[...] + product_rows * inv_snp,
        inverse[...],
        (((1,), (1,)), ((), ())),
        precision=lax.Precision.HIGHEST,
        preferred_element_type=jnp.float32,
    )


def panel(pick, old, inverse, parts, shards):
    count = shards[0].shape[0]
    block = pl.BlockSpec((ROW_STEP, NB), lambda i, t: (t[1 + i], 0))
    return pl.pallas_call(
        lambda *refs: panel_kernel(*refs, inv_snp=1.0 / count),
        grid_spec=pltpu.PrefetchScalarGridSpec(
            num_scalar_prefetch=1,
            grid=(4,),
            in_specs=[
                block,
                pl.BlockSpec((NB, NB), lambda i, t: (0, 0)),
                *[pl.BlockSpec(memory_space=pl.ANY)] * 26,
            ],
            out_specs=block,
            scratch_shapes=[
                pltpu.VMEM((2, ROW_STEP, count), jnp.bfloat16),
                pltpu.VMEM((count, NB), jnp.bfloat16),
                pltpu.SemaphoreType.DMA((2, 4)),
                pltpu.SemaphoreType.DMA(()),
            ],
        ),
        out_shape=jax.ShapeDtypeStruct((4 * ROW_STEP, NB), jnp.float32),
        name="panel",
    )(pick, old, inverse, *parts, *shards)


def unpack_kernel(coded, *refs):
    out = refs[-1]
    for source in range(4):
        code = coded[source, TILE_ROWS * HALF :, :].astype(jnp.float32)
        scale = jnp.exp(code * LOG_STEP) * (1.0 / LEVELS)
        for a in range(PAIRS):
            values = coded[source, a * 16 : (a + 1) * 16, :].astype(jnp.float32) * scale
            row = source * TILE_ROWS + a * 2
            out[row : row + 2] = values.reshape(2, HALF, 128)


def unpack(part, coded, before):
    begun = [] if before is None else [before]
    return pl.pallas_call(
        unpack_kernel,
        grid=(4,),
        in_specs=[
            pl.BlockSpec((4, CODED_ROWS, 128), lambda i: (i, 0, 0)),
            *[pl.BlockSpec(memory_space=pl.ANY)] * len(begun),
        ],
        out_specs=pl.BlockSpec((4 * TILE_ROWS, HALF, 128), lambda i: (i, part, 0)),
        out_shape=jax.ShapeDtypeStruct((16 * TILE_ROWS, 2 * HALF, 128), jnp.float32),
        input_output_aliases={1: 0} if begun else {},
        name="unpack",
    )(coded, *begun)


def compute(genotypes, running, grid_map):
    row_index = lax.axis_index("row").astype(jnp.uint32)
    col_index = lax.axis_index("col").astype(jnp.uint32)
    z, x_lo, core = row_index >> 2, (row_index >> 1) & 1, row_index & 1
    y, x_hi = col_index >> 1, col_index & 1
    snp_count = genotypes.shape[0]
    inv_snp = 1.0 / snp_count

    def dot0(a, b):
        return lax.dot_general(a, b, (((0,), (0,)), ((), ())), preferred_element_type=jnp.float32)

    def twin(value):
        return lax.ppermute(value, "row", row_perm(0, 0, 1))

    turned = genotypes.T
    across = lax.ppermute(turned, "col", col_perm(0, 1))
    z_up, z_down = ring_sides(genotypes, "row", row_perm)
    y_up, y_down = ring_sides(turned, "col", col_perm)
    own_twin = twin(genotypes)

    leading = running[:NB, 0, 0, :] + dot0(genotypes, genotypes) * inv_snp
    lower = jnp.linalg.cholesky(leading)

    away = (jnp.arange(4, dtype=jnp.uint32) - z) & 3
    slots = jnp.where(away == 0, 0, jnp.where(away == 1, 2, jnp.where(away == 2, 3, 1)))
    slots = slots.astype(jnp.int32)
    pick = slots[0] * 4 + (core * 2 + x_lo).astype(jnp.int32)
    pick = jnp.stack([pick, *[jnp.int32(step) for step in STEP_OF_SLOT]])

    late, across, lower, pick, slots = lax.optimization_barrier(
        (genotypes, across, lower, pick, slots)
    )
    beside = lax.ppermute(late, "row", row_perm(0, 1, 0))
    y_up_across, y_down_across = ring_sides(across, "col", col_perm)
    z_opposite = jnp.concatenate(ring_relay(z_up, z_down, "row", row_perm), axis=0)
    y_opposite = ring_relay(y_up, y_down, "col", col_perm)
    z_up_twin, z_down_twin = twin(z_up), twin(z_down)

    inverse = lax.linalg.triangular_solve(
        lower, jnp.eye(NB, dtype=jnp.float32), left_side=True, lower=True
    )
    heard = sum(lax.ppermute(inverse, "row", [(0, d * NX * NC)]) for d in range(1, NZ))
    inverse = jnp.where(z == 0, inverse, heard)
    z_up_side, z_down_side = ring_sides(beside, "row", row_perm)
    heard = lax.ppermute(inverse, "row", [(d * NX * NC, d * NX * NC + NC) for d in range(NZ)])
    heard, old_panel = lax.optimization_barrier((heard, running[:, 0, 0, :]))
    inverse = jnp.where(x_lo == 0, inverse, heard)
    z_opposite_side = lax.ppermute(z_opposite, "row", row_perm(0, 1, 0))
    y_opposite_across = ring_relay(y_up_across, y_down_across, "col", col_perm)
    heard = lax.ppermute(inverse, "row", [(d * NC, d * NC + 1) for d in range(NZ * NX)])
    inverse = jnp.where(core == 0, inverse, heard)

    row_parts = [turned, across, y_up, y_up_across, y_down, y_down_across]
    row_parts += [*y_opposite, *y_opposite_across]
    col_shards = [
        (genotypes, beside, own_twin, twin(beside)),
        (z_up, z_up_side, z_up_twin, twin(z_up_side)),
        (z_down, z_down_side, z_down_twin, twin(z_down_side)),
        (z_opposite, z_opposite_side, twin(z_opposite), twin(z_opposite_side)),
    ]

    flat_shards = [shard for group in col_shards for shard in group]
    factor = panel(pick, old_panel, inverse, row_parts, flat_shards)
    pieces = factor.reshape(NY, NH, 128, NB)
    heard = lax.ppermute(pieces[:, 1], "col", [(0, 1)])
    pieces = jnp.where(x_hi == 0, pieces[:, 0], heard)
    heard = sum(
        lax.ppermute(pieces[d], "col", [(h, d * NH + h) for h in range(NH)]) for d in range(1, NY)
    )
    own_factor = jnp.where(y == 0, pieces[0], heard)
    pair = jnp.stack([own_factor, lax.ppermute(own_factor, "col", col_perm(0, 1))])
    row_factor = jnp.concatenate(ring_direct(pair, "col", col_perm), axis=0).reshape(1024, NB)
    pair = jnp.stack([own_factor, lax.ppermute(own_factor, "row", row_perm(0, 1, 0))])
    half = jnp.stack(ring_direct(pair, "row", row_perm))
    half_twin = lax.ppermute(half, "row", row_perm(0, 0, 1))
    high, low = split_bf16(jnp.stack([half, half_twin], axis=1).reshape(2048, NB).T)
    col_factor = jnp.concatenate([high, low, high], axis=0)

    tiles = jnp.arange(16, dtype=jnp.uint32)
    hit = grid_map[None, :] == jnp.arange(16, dtype=jnp.int32)[:, None]
    inverse_map = jnp.sum(jnp.where(hit, tiles[None, :], 0), axis=1).astype(jnp.uint32)
    step_y = ((inverse_map >> 2) - y) & 3
    slot = jnp.where(step_y == 0, 0, jnp.where(step_y == 1, 2, jnp.where(step_y == 2, 3, 1)))
    tile = ((slot.astype(jnp.uint32) * 2) + (((inverse_map >> 1) & 1) ^ x_hi)) * 2 + (inverse_map & 1)
    row_start = row_index * 1024 + inverse_map * 64
    side = jnp.arange(4, dtype=jnp.uint32)
    place = (((side & 1) ^ x_lo) << 1) + ((side >> 1) ^ core)
    is_col0 = jnp.where(col_index == 0, 1, 0).astype(jnp.uint32)
    table = jnp.concatenate(
        [inverse_map, tile, row_start, place, slots.astype(jnp.uint32), is_col0[None]]
    ).astype(jnp.int32)

    prods = []
    running = running.reshape(1024, 16, 128)
    late_rows, factor = lax.optimization_barrier((row_parts, factor))
    for plane in range(3):
        prods.append(product(plane, slots, late_rows, flat_shards))
    result = None
    for part in range(2):
        if part == 1:
            late_rows, packed = lax.optimization_barrier((row_parts, packed))
            prods.append(product(3, slots, late_rows, flat_shards))
        packed = epilogue(
            part, table, running, prods[2 * part : 2 * part + 2], row_factor, col_factor, snp_count
        )
        coded = lax.all_to_all(
            packed.reshape(16, CODED_ROWS, 128), "row", split_axis=0, concat_axis=0, tiled=True
        )
        result = unpack(part, coded, result)
    return result.reshape(16, 1, 64, 16, 1, 128)


def solution(mesh):
    in_specs = (P(None, ("row", "col")), P("row", None, "col", None), P())
    out_specs = P(None, "row", None, None, "col", None)
    return jax.shard_map(
        compute, mesh=mesh, in_specs=in_specs, out_specs=out_specs, check_vma=False
    )
```

```python
import jax
import jax.numpy as jnp
from jax import lax
from jax.experimental import pallas as pl
from jax.experimental.pallas import tpu as pltpu
from jax.sharding import PartitionSpec as P


NB = 128
NZ, NX, NC = 4, 2, 2
NY, NH = 4, 2
STEP_OF_SLOT = (0, 3, 1, 2)
TILE_ROWS = 64
HALF = 8
PAIRS = TILE_ROWS * HALF // 16
TILES_STEP = 2
CODED_ROWS = TILE_ROWS * HALF + 16
LEVELS = 32767.0
LOG_STEP = 0.6931471805599453 / 64.0


def row_perm(dz=0, fx=0, fc=0):
    return [
        ((z * NX + x) * NC + k, (((z + dz) % NZ) * NX + (x ^ fx)) * NC + (k ^ fc))
        for z in range(NZ)
        for x in range(NX)
        for k in range(NC)
    ]


def col_perm(dy=0, fh=0):
    return [(y * NH + h, ((y + dy) % NY) * NH + (h ^ fh)) for y in range(NY) for h in range(NH)]


def ring_sides(shard, axis, perm):
    return lax.ppermute(shard, axis, perm(1)), lax.ppermute(shard, axis, perm(-1))


def ring_relay(up, down, axis, perm):
    half = up.shape[0] // 2
    top = lax.ppermute(up[:half], axis, perm(1))
    bottom = lax.ppermute(down[half:], axis, perm(-1))
    return top, bottom


def ring_direct(shard, axis, perm):
    return [shard] + [lax.ppermute(shard, axis, perm(d)) for d in (1, -1, 2)]


def split_bf16(value):
    high = lax.reduce_precision(value, exponent_bits=8, mantissa_bits=7)
    return high.astype(jnp.bfloat16), (value - high).astype(jnp.bfloat16)


def epilogue_kernel(table, *refs, part, inv_snp):
    tiles, (col_factor0, col_factor1, out, values) = refs[: 4 * TILES_STEP], refs[4 * TILES_STEP :]
    for n in range(TILES_STEP):
        running, prod0, prod1, row_factor = tiles[n * 4 : (n + 1) * 4]
        row_start = table[32 + pl.program_id(0) * TILES_STEP + n]
        old_rows = running.reshape(TILE_ROWS * HALF, 128)
        mine = row_factor[...]
        high = mine.astype(jnp.bfloat16)
        low = (mine - high.astype(jnp.float32)).astype(jnp.bfloat16)
        left = jnp.concatenate([high, high, low], axis=1)
        for plane, (prod, col_factor) in enumerate(((prod0, col_factor0), (prod1, col_factor1))):
            outer = jnp.dot(left, col_factor[...], preferred_element_type=jnp.float32)
            for side in range(4):
                place = table[48 + side] + plane * 4
                lanes = slice(side * 128, (side + 1) * 128)
                old = old_rows[pl.ds(place, TILE_ROWS, stride=HALF), :]
                values[n, pl.ds(place, TILE_ROWS, stride=HALF), :] = (
                    old + prod[:, lanes] * inv_snp - outer[:, lanes]
                )

        @pl.when(row_start < NB)
        def _():
            values[n] = jnp.zeros((TILE_ROWS * HALF, 128), jnp.float32)

        if part == 0:

            @pl.when(table[56] == 1)
            def _():
                row_pos = row_start + lax.broadcasted_iota(jnp.int32, (TILE_ROWS, NB), 0)
                lane = lax.broadcasted_iota(jnp.int32, (TILE_ROWS, NB), 1)
                values[n, pl.ds(0, TILE_ROWS, stride=HALF), :] = jnp.where(
                    row_pos >= lane, mine, 0.0
                )

    for n in range(TILES_STEP):
        peak = jnp.full((16, 128), 1e-30, jnp.float32)
        for a in range(PAIRS):
            peak = jnp.maximum(peak, jnp.abs(values[n, a * 16 : (a + 1) * 16, :]))
        peak = jnp.maximum(peak[:8], peak[8:])
        code = jnp.minimum(jnp.ceil(jnp.log(peak) * (1.0 / LOG_STEP)) + 1.0, 8190.0)
        code = jnp.concatenate([code, code], axis=0)
        gain = LEVELS / jnp.exp(code * LOG_STEP)
        base = n * CODED_ROWS
        for a in range(PAIRS):
            scaled = jnp.round(values[n, a * 16 : (a + 1) * 16, :] * gain)
            out[base + a * 16 : base + (a + 1) * 16, :] = scaled.astype(jnp.int32).astype(jnp.int16)
        last = base + TILE_ROWS * HALF
        out[last : last + 16, :] = code.astype(jnp.int32).astype(jnp.int16)


def epilogue(part, table, running, prods, row_factor, col_factor, snp_count):
    specs, arrays = [], []
    for n in range(TILES_STEP):
        block = pl.BlockSpec((TILE_ROWS, 512), lambda i, t, n=n: (t[16 + i * TILES_STEP + n], 0))
        specs += [
            pl.BlockSpec(
                (TILE_ROWS, HALF, 128), lambda i, t, n=n: (t[i * TILES_STEP + n], part, 0)
            ),
            block,
            block,
            pl.BlockSpec((TILE_ROWS, NB), lambda i, t, n=n: (t[16 + i * TILES_STEP + n], 0)),
        ]
        arrays += [running, *prods, row_factor]
    return pl.pallas_call(
        lambda *refs: epilogue_kernel(*refs, part=part, inv_snp=1.0 / snp_count),
        grid_spec=pltpu.PrefetchScalarGridSpec(
            num_scalar_prefetch=1,
            grid=(16 // TILES_STEP,),
            in_specs=[
                *specs,
                pl.BlockSpec((3 * NB, 512), lambda i, t: (0, t[52 + part * 2])),
                pl.BlockSpec((3 * NB, 512), lambda i, t: (0, t[53 + part * 2])),
            ],
            out_specs=pl.BlockSpec((TILES_STEP * CODED_ROWS, 128), lambda i, t: (i, 0)),
            scratch_shapes=[pltpu.VMEM((TILES_STEP, TILE_ROWS * HALF, 128), jnp.float32)],
        ),
        out_shape=jax.ShapeDtypeStruct((16 * CODED_ROWS, 128), jnp.int16),
        name="epilogue",
    )(table, *arrays, col_factor, col_factor)


ROW_STEP = 256
ROW_PLACES = ((0, 0, 0), (0, 1, 128), (1, 2, 0), (1, 3, 128), (2, 4, 0), (2, 5, 128))
ROW_PLACES += ((3, 6, 0), (3, 7, 64), (3, 8, 128), (3, 9, 192))


def fetch_rows(parts, rows, sems):
    step = pl.program_id(0)

    def copies(n):
        places = [(part, row) for where, part, row in ROW_PLACES if where == n]
        return [
            pltpu.make_async_copy(
                parts[part],
                rows.at[n % 2, row : row + parts[part].shape[0], :],
                sems.at[n % 2, number],
            )
            for number, (part, row) in enumerate(places)
        ]

    for n in range(4):

        @pl.when(step == n)
        def _():
            if n == 0:
                for copy in copies(0):
                    copy.start()
            if n < 3:
                for copy in copies(n + 1):
                    copy.start()
            for copy in copies(n):
                copy.wait()


def product_kernel(slots, *refs, plane):
    parts, shards, (out, rows, cols, row_sems, col_sems) = refs[:10], refs[10:26], refs[26:]
    first = pl.program_id(0) == 0

    def copy(slot, side):
        return pltpu.make_async_copy(
            shards[slot * 4 + side], cols.at[:, side * 128 : (side + 1) * 128], col_sems.at[side]
        )

    for slot in range(4):

        @pl.when(jnp.logical_and(first, slots[plane] == slot))
        def _():
            for side in range(4):
                copy(slot, side).start()

    fetch_rows(parts, rows, row_sems)

    @pl.when(first)
    def _():
        for side in range(4):
            copy(0, side).wait()

    out[...] = jnp.dot(
        rows[pl.program_id(0) % 2], cols[...], preferred_element_type=jnp.float32
    )


def product(plane, slots, parts, shards):
    count = shards[0].shape[0]
    return pl.pallas_call(
        lambda *refs: product_kernel(*refs, plane=plane),
        grid_spec=pltpu.PrefetchScalarGridSpec(
            num_scalar_prefetch=1,
            grid=(4,),
            in_specs=[pl.BlockSpec(memory_space=pl.ANY)] * 26,
            out_specs=pl.BlockSpec((ROW_STEP, 512), lambda i, t: (i, 0)),
            scratch_shapes=[
                pltpu.VMEM((2, ROW_STEP, count), jnp.bfloat16),
                pltpu.VMEM((count, 512), jnp.bfloat16),
                pltpu.SemaphoreType.DMA((2, 4)),
                pltpu.SemaphoreType.DMA((4,)),
            ],
        ),
        out_shape=jax.ShapeDtypeStruct((4 * ROW_STEP, 512), jnp.float32),
        name="product",
    )(slots, *parts, *shards)


def panel_kernel(pick, old, inverse, *refs, inv_snp):
    parts, shards, (out, rows, first, row_sems, sem) = refs[:10], refs[10:26], refs[26:]

    @pl.when(pl.program_id(0) == 0)
    def _():
        for n in range(16):

            @pl.when(pick[0] == n)
            def _():
                pltpu.make_async_copy(shards[n], first, sem).start()

    fetch_rows(parts, rows, row_sems)

    @pl.when(pl.program_id(0) == 0)
    def _():
        pltpu.make_async_copy(shards[0], first, sem).wait()

    product_rows = jnp.dot(
        rows[pl.program_id(0) % 2], first[...], preferred_element_type=jnp.float32
    )
    out[...] = lax.dot_general(
        old[...] + product_rows * inv_snp,
        inverse[...],
        (((1,), (1,)), ((), ())),
        precision=lax.Precision.HIGHEST,
        preferred_element_type=jnp.float32,
    )


def panel(pick, old, inverse, parts, shards):
    count = shards[0].shape[0]
    block = pl.BlockSpec((ROW_STEP, NB), lambda i, t: (t[1 + i], 0))
    return pl.pallas_call(
        lambda *refs: panel_kernel(*refs, inv_snp=1.0 / count),
        grid_spec=pltpu.PrefetchScalarGridSpec(
            num_scalar_prefetch=1,
            grid=(4,),
            in_specs=[
                block,
                pl.BlockSpec((NB, NB), lambda i, t: (0, 0)),
                *[pl.BlockSpec(memory_space=pl.ANY)] * 26,
            ],
            out_specs=block,
            scratch_shapes=[
                pltpu.VMEM((2, ROW_STEP, count), jnp.bfloat16),
                pltpu.VMEM((count, NB), jnp.bfloat16),
                pltpu.SemaphoreType.DMA((2, 4)),
                pltpu.SemaphoreType.DMA(()),
            ],
        ),
        out_shape=jax.ShapeDtypeStruct((4 * ROW_STEP, NB), jnp.float32),
        name="panel",
    )(pick, old, inverse, *parts, *shards)


def unpack_kernel(coded, *refs):
    out = refs[-1]
    for source in range(8):
        code = coded[source, TILE_ROWS * HALF :, :].astype(jnp.float32)
        scale = jnp.exp(code * LOG_STEP) * (1.0 / LEVELS)
        for a in range(PAIRS):
            values = coded[source, a * 16 : (a + 1) * 16, :].astype(jnp.float32) * scale
            row = source * TILE_ROWS + a * 2
            out[row : row + 2] = values.reshape(2, HALF, 128)


def unpack(part, coded, before):
    begun = [] if before is None else [before]
    return pl.pallas_call(
        unpack_kernel,
        grid=(2,),
        in_specs=[
            pl.BlockSpec((8, CODED_ROWS, 128), lambda i: (i, 0, 0)),
            *[pl.BlockSpec(memory_space=pl.ANY)] * len(begun),
        ],
        out_specs=pl.BlockSpec((8 * TILE_ROWS, HALF, 128), lambda i: (i, part, 0)),
        out_shape=jax.ShapeDtypeStruct((16 * TILE_ROWS, 2 * HALF, 128), jnp.float32),
        input_output_aliases={1: 0} if begun else {},
        name="unpack",
    )(coded, *begun)


def compute(genotypes, running, grid_map):
    row_index = lax.axis_index("row").astype(jnp.uint32)
    col_index = lax.axis_index("col").astype(jnp.uint32)
    z, x_lo, core = row_index >> 2, (row_index >> 1) & 1, row_index & 1
    y, x_hi = col_index >> 1, col_index & 1
    snp_count = genotypes.shape[0]
    inv_snp = 1.0 / snp_count

    def dot0(a, b):
        return lax.dot_general(a, b, (((0,), (0,)), ((), ())), preferred_element_type=jnp.float32)

    def twin(value):
        return lax.ppermute(value, "row", row_perm(0, 0, 1))

    turned = genotypes.T
    across = lax.ppermute(turned, "col", col_perm(0, 1))
    z_up, z_down = ring_sides(genotypes, "row", row_perm)
    y_up, y_down = ring_sides(turned, "col", col_perm)
    own_twin = twin(genotypes)

    leading = running[:NB, 0, 0, :] + dot0(genotypes, genotypes) * inv_snp
    lower = jnp.linalg.cholesky(leading)

    away = (jnp.arange(4, dtype=jnp.uint32) - z) & 3
    slots = jnp.where(away == 0, 0, jnp.where(away == 1, 2, jnp.where(away == 2, 3, 1)))
    slots = slots.astype(jnp.int32)
    pick = slots[0] * 4 + (core * 2 + x_lo).astype(jnp.int32)
    pick = jnp.stack([pick, *[jnp.int32(step) for step in STEP_OF_SLOT]])

    late, across, lower, pick, slots = lax.optimization_barrier(
        (genotypes, across, lower, pick, slots)
    )
    beside = lax.ppermute(late, "row", row_perm(0, 1, 0))
    y_up_across, y_down_across = ring_sides(across, "col", col_perm)
    z_opposite = jnp.concatenate(ring_relay(z_up, z_down, "row", row_perm), axis=0)
    y_opposite = ring_relay(y_up, y_down, "col", col_perm)
    z_up_twin, z_down_twin = twin(z_up), twin(z_down)

    inverse = lax.linalg.triangular_solve(
        lower, jnp.eye(NB, dtype=jnp.float32), left_side=True, lower=True
    )
    heard = sum(lax.ppermute(inverse, "row", [(0, d * NX * NC)]) for d in range(1, NZ))
    inverse = jnp.where(z == 0, inverse, heard)
    z_up_side, z_down_side = ring_sides(beside, "row", row_perm)
    heard = lax.ppermute(inverse, "row", [(d * NX * NC, d * NX * NC + NC) for d in range(NZ)])
    heard, old_panel = lax.optimization_barrier((heard, running[:, 0, 0, :]))
    inverse = jnp.where(x_lo == 0, inverse, heard)
    z_opposite_side = lax.ppermute(z_opposite, "row", row_perm(0, 1, 0))
    y_opposite_across = ring_relay(y_up_across, y_down_across, "col", col_perm)
    heard = lax.ppermute(inverse, "row", [(d * NC, d * NC + 1) for d in range(NZ * NX)])
    inverse = jnp.where(core == 0, inverse, heard)

    row_parts = [turned, across, y_up, y_up_across, y_down, y_down_across]
    row_parts += [*y_opposite, *y_opposite_across]
    col_shards = [
        (genotypes, beside, own_twin, twin(beside)),
        (z_up, z_up_side, z_up_twin, twin(z_up_side)),
        (z_down, z_down_side, z_down_twin, twin(z_down_side)),
        (z_opposite, z_opposite_side, twin(z_opposite), twin(z_opposite_side)),
    ]

    flat_shards = [shard for group in col_shards for shard in group]
    factor = panel(pick, old_panel, inverse, row_parts, flat_shards)
    pieces = factor.reshape(NY, NH, 128, NB)
    heard = lax.ppermute(pieces[:, 1], "col", [(0, 1)])
    pieces = jnp.where(x_hi == 0, pieces[:, 0], heard)
    heard = sum(
        lax.ppermute(pieces[d], "col", [(h, d * NH + h) for h in range(NH)]) for d in range(1, NY)
    )
    own_factor = jnp.where(y == 0, pieces[0], heard)
    pair = jnp.stack([own_factor, lax.ppermute(own_factor, "col", col_perm(0, 1))])
    row_factor = jnp.concatenate(ring_direct(pair, "col", col_perm), axis=0).reshape(1024, NB)
    pair = jnp.stack([own_factor, lax.ppermute(own_factor, "row", row_perm(0, 1, 0))])
    half = jnp.stack(ring_direct(pair, "row", row_perm))
    half_twin = lax.ppermute(half, "row", row_perm(0, 0, 1))
    high, low = split_bf16(jnp.stack([half, half_twin], axis=1).reshape(2048, NB).T)
    col_factor = jnp.concatenate([high, low, high], axis=0)

    tiles = jnp.arange(16, dtype=jnp.uint32)
    hit = grid_map[None, :] == jnp.arange(16, dtype=jnp.int32)[:, None]
    inverse_map = jnp.sum(jnp.where(hit, tiles[None, :], 0), axis=1).astype(jnp.uint32)
    step_y = ((inverse_map >> 2) - y) & 3
    slot = jnp.where(step_y == 0, 0, jnp.where(step_y == 1, 2, jnp.where(step_y == 2, 3, 1)))
    tile = ((slot.astype(jnp.uint32) * 2) + (((inverse_map >> 1) & 1) ^ x_hi)) * 2 + (inverse_map & 1)
    row_start = row_index * 1024 + inverse_map * 64
    side = jnp.arange(4, dtype=jnp.uint32)
    place = (((side & 1) ^ x_lo) << 1) + ((side >> 1) ^ core)
    is_col0 = jnp.where(col_index == 0, 1, 0).astype(jnp.uint32)
    table = jnp.concatenate(
        [inverse_map, tile, row_start, place, slots.astype(jnp.uint32), is_col0[None]]
    ).astype(jnp.int32)

    prods = []
    running = running.reshape(1024, 16, 128)
    late_rows, factor = lax.optimization_barrier((row_parts, factor))
    for plane in range(3):
        prods.append(product(plane, slots, late_rows, flat_shards))
    result = None
    for part in range(2):
        if part == 1:
            late_rows, packed = lax.optimization_barrier((row_parts, packed))
            prods.append(product(3, slots, late_rows, flat_shards))
        packed = epilogue(
            part, table, running, prods[2 * part : 2 * part + 2], row_factor, col_factor, snp_count
        )
        coded = lax.all_to_all(
            packed.reshape(16, CODED_ROWS, 128), "row", split_axis=0, concat_axis=0, tiled=True
        )
        result = unpack(part, coded, result)
    return result.reshape(16, 1, 64, 16, 1, 128)


def solution(mesh):
    in_specs = (P(None, ("row", "col")), P("row", None, "col", None), P())
    out_specs = P(None, "row", None, None, "col", None)
    return jax.shard_map(
        compute, mesh=mesh, in_specs=in_specs, out_specs=out_specs, check_vma=False
    )
```
